32 devices in a mesh: pole: 4 (over x, core), row: 4 (over z), col: 2 (over y).
Axes of the slice: x: 2, y: 2, z: 4, core: 2. Of those that a mesh axis runs over, the one named last changes fastest.
Arguments:
- green: bfloat16 [4, 4096, 4096], P('pole', 'row', 'col'), may hold values from -6 to 6
- factor: bfloat16 [4, 4096, 1024], P('pole', 'row', 'col'), may hold values from -0.09375 to 0.09375
- diag_inverse: bfloat16 [4, 512, 1024], P('pole', 'row', 'col'), may hold values from -6 to 6
- pole_weight: float32 [4], P('pole'), may hold values from 0.25 to 1
- pattern: int32 [8, 2], replicated, may hold values 0 or 1
Outputs:
- off_density: float32 [4096, 1024], P(('row', 'pole'), 'col')
- diag_density: float32 [512, 1024], P(('pole', 'row'), 'col')
The draws below stay inside these ranges and needn't reach their ends.
All inputs are finite; a program needn't handle non-finite values.
Results may differ from the reference program's by a relative error of at most 0.005.
Values may be sent and summed in bfloat16 or wider, within the bound.
No kernel may reach another device: no remote copies, remote signals or barrier semaphores. Data moves between devices by JAX's collectives and lax.ppermute only.
A program may use at most 64 MiB of HBM per device.

```python
import math
import jax
import jax.numpy as jnp

BLOCK = 512
ANC = 8
POLES = 4
KS = 2


def touch_ends(values, rng, least, high):
    index_at = [jax.random.randint(jax.random.fold_in(rng, axis), (), 0, length) for axis, length in enumerate(values.shape)]
    longest = values.shape.index(max(values.shape))
    beside = index_at[:longest] + [(index_at[longest] + 1) % values.shape[longest]] + index_at[longest + 1:]
    return values.at[tuple(index_at)].set(least).at[tuple(beside)].set(high)


def block_levels(own_key, extent, split, least, high):
    def one(dim, parts):
        steps = jax.random.uniform(jax.random.fold_in(jax.random.fold_in(own_key, 6), dim), (parts,), jnp.float32, least / len(split), high / len(split))
        return jnp.repeat(jnp.exp(steps), extent[dim] // parts).reshape((-1,) + (1,) * (len(extent) - dim - 1))

    loudness = one(*split[0])
    for cut in split[1:]:
        loudness = loudness * one(*cut)
    return loudness


def scatter_about(own_key, shape, scale, most, split=(), held_as=jnp.bfloat16):
    array = scale * jax.random.normal(own_key, shape, jnp.float32)
    if split:
        array = array * block_levels(own_key, shape, split, -0.22, 0.18)
    return jnp.clip(array, -most, most).astype(held_as)


def setup_inputs(seed: int = 0) -> dict:
    arg_keys = jax.random.split(jax.random.key(seed), 6)
    return {
        "green": scatter_about(arg_keys[0], (POLES, ANC * BLOCK, ANC * BLOCK), 1.0, 6.0, ((0, 4), (1, 4), (2, 2))),
        "factor": scatter_about(arg_keys[1], (POLES, ANC * BLOCK, KS * BLOCK), (ANC * BLOCK) ** -0.5, 0.09375, ((0, 4), (1, 4), (2, 2))),
        "diag_inverse": scatter_about(arg_keys[2], (POLES, BLOCK, KS * BLOCK), 1.0, 6.0, ((0, 4), (1, 4), (2, 2))),
        "pole_weight": jnp.clip(jnp.exp(math.log(1.0) - 1.3862944 * jax.random.uniform(arg_keys[3], (POLES,), jnp.float32) ** block_levels(arg_keys[3], (POLES,), ((0, 4),), -0.2, 0.2)), 0.25, 1.0),
        "pattern": touch_ends((jax.random.randint(arg_keys[4], (ANC, KS), 0, 2) < 1).astype(jnp.int32), jax.random.fold_in(arg_keys[4], 1), 0, 1),
    }


def reference(green, factor, diag_inverse, pole_weight, pattern):
    pattern_f = pattern.astype(jnp.float32)
    keep_mask = jnp.repeat(jnp.repeat(pattern_f, BLOCK, axis=0), BLOCK, axis=1)
    masked = factor * keep_mask.astype(jnp.bfloat16)[None]
    off_density = jnp.zeros((ANC * BLOCK, KS * BLOCK), jnp.float32)
    diag_density = jnp.zeros((BLOCK, KS * BLOCK), jnp.float32)
    for pole_at in range(POLES):
        product = jnp.dot(green[pole_at], masked[pole_at], preferred_element_type=jnp.float32)
        update = (product * keep_mask).astype(jnp.bfloat16)
        off_density = off_density - pole_weight[pole_at] * update.astype(jnp.float32)
        factor_split = masked[pole_at].astype(jnp.float32).reshape(ANC * BLOCK, KS, BLOCK)
        update_split = update.astype(jnp.float32).reshape(ANC * BLOCK, KS, BLOCK)
        cross_term = jnp.einsum("rka,rkb->akb", factor_split, update_split).reshape(BLOCK, KS * BLOCK)
        diag_density = diag_density + pole_weight[pole_at] * (diag_inverse[pole_at].astype(jnp.float32) - cross_term)
    return off_density, diag_density
```

```python
import jax
import jax.numpy as jnp
from jax import lax
from jax.sharding import PartitionSpec as P


def swap_sum(part, axis, size, group, stride, held_as):
    at = lax.axis_index(axis)
    digit = (at // stride) % group
    total = lax.dynamic_index_in_dim(part, digit, 0, keepdims=False)
    for step in range(1, group):
        perm = []
        for i in range(size):
            d = (i // stride) % group
            perm.append((i, i + ((d + step) % group - d) * stride))
        to = (digit + step) % group
        send = lax.dynamic_index_in_dim(part, to, 0, keepdims=False).astype(held_as)
        total = total + lax.ppermute(send, axis, perm).astype(jnp.float32)
    return total


def make_body(mesh):
    poles_n, rows_n, cols_n = (mesh.shape[a] for a in ("pole", "row", "col"))

    def body(green, factor, diag_inverse, pole_weight, pattern):
        local_rows, k_local = green.shape[1], green.shape[2]
        cols = factor.shape[2]
        anc, supers = pattern.shape
        block = local_rows * rows_n // anc
        per_row = local_rows // block
        per_col = k_local // block
        row_at = lax.axis_index("row")
        col_at = lax.axis_index("col")
        level = cols // block
        pattern_f = pattern.astype(jnp.float32)
        here = lax.dynamic_slice(pattern_f, (0, col_at * level), (anc, level))
        keep = jnp.repeat(here, block, axis=1)
        own_keep = lax.dynamic_slice_in_dim(keep, row_at * per_row, per_row, 0)

        weight = pole_weight[0]
        gl = green[0]
        fac = factor[0].reshape(per_row, block, cols)

        got = {}
        for shift in range(1, cols_n):
            perm = [(i, (i + shift) % cols_n) for i in range(cols_n)]
            for j in range(per_col):
                got[shift, j] = lax.ppermute(gl[:, j * block:(j + 1) * block], "col", perm)

        right = [(i, i + 1) for i in range(rows_n - 1)]
        left = [(i + 1, i) for i in range(rows_n - 1)]
        from_left, from_right = {}, {}
        for e in range(per_row):
            a = b = fac[e]
            for step in range(1, rows_n):
                a = lax.ppermute(a, "row", right)
                b = lax.ppermute(b, "row", left)
                from_left[step, e] = a
                from_right[step, e] = b
        blocks = {(0, e): fac[e] for e in range(per_row)}
        for step in range(1, rows_n):
            for e in range(per_row):
                blocks[step, e] = jnp.where(row_at >= step, from_left[step, e], from_right[rows_n - step, e])
        stacked = jnp.stack([blocks[s, e] for s in range(rows_n) for e in range(per_row)])

        def factor_of(a):
            row = a // per_row
            at = ((row_at - row) % rows_n) * per_row + a % per_row
            kept = lax.dynamic_index_in_dim(keep, a, 0).astype(jnp.bfloat16)
            return lax.dynamic_index_in_dim(stacked, at, 0, keepdims=False) * kept

        product = jnp.zeros((local_rows, cols), jnp.float32)
        for j in range(per_col):
            product += jnp.dot(gl[:, j * block:(j + 1) * block], factor_of(col_at * per_col + j),
                               preferred_element_type=jnp.float32)
        for shift in range(1, cols_n):
            for j in range(per_col):
                src = (col_at - shift) % cols_n
                product += jnp.dot(got[shift, j], factor_of(src * per_col + j),
                                   preferred_element_type=jnp.float32)
        product = (product.reshape(per_row, block, cols) * own_keep[:, None, :])
        update = product.astype(jnp.bfloat16).reshape(local_rows, level, block)
        masked = (fac * own_keep.astype(jnp.bfloat16)[:, None, :]).reshape(local_rows, level, block)
        cross = jnp.einsum("rka,rkb->akb", masked, update, preferred_element_type=jnp.float32).reshape(block, cols)
        diag = -weight * cross
        count = diag_inverse.shape[1]
        mine = lax.dynamic_slice_in_dim(diag, row_at * count, count, 0) + weight * diag_inverse[0].astype(jnp.float32)
        diag = lax.dynamic_update_slice_in_dim(diag, mine, row_at * count, 0)
        off = -weight * product.reshape(local_rows, cols)

        cores = 2 if poles_n % 2 == 0 else 1
        outer = poles_n // cores
        res = []
        for x in (diag, off):
            r = x.shape[0] // poles_n
            x = x.reshape(outer, cores, r, cols).transpose(1, 0, 2, 3)
            if cores > 1:
                x = swap_sum(x, "pole", poles_n, cores, 1, jnp.bfloat16)
            else:
                x = x[0]
            res.append(swap_sum(x, "pole", poles_n, outer, cores, jnp.bfloat16))
        diag, off = res
        diag = swap_sum(diag.reshape(rows_n, -1, cols), "row", rows_n, rows_n, 1, jnp.bfloat16)
        return off, diag

    return body


def solution(mesh):
    in_specs = (
        P("pole", "row", "col"),
        P("pole", "row", "col"),
        P("pole", "row", "col"),
        P("pole"),
        P(),
    )
    out_specs = (P(("row", "pole"), "col"), P(("pole", "row"), "col"))
    return jax.shard_map(make_body(mesh), mesh=mesh, in_specs=in_specs, out_specs=out_specs, check_vma=False)
```

```python
import functools

import jax
import jax.numpy as jnp
from jax import lax
from jax.experimental import pallas as pl
from jax.experimental.pallas import tpu as pltpu
from jax.sharding import PartitionSpec as P


VMEM = pl.BlockSpec(memory_space=pltpu.VMEM)
SMEM = pl.BlockSpec(memory_space=pltpu.SMEM)
ANY = pl.BlockSpec(memory_space=pl.ANY)
F32 = jnp.float32
BF16 = jnp.bfloat16


class Sizes:
    def __init__(self, mesh, green, factor, diag_inverse, pattern):
        self.poles, self.rows, self.cols = (mesh.shape[a] for a in ("pole", "row", "col"))
        self.local_rows, self.k_local = green.shape[1], green.shape[2]
        self.width = factor.shape[2]
        self.anc, supers = pattern.shape
        self.block = self.local_rows * self.rows // self.anc
        self.per_row = self.local_rows // self.block
        self.half = self.k_local // self.block
        self.level = supers // self.cols
        self.count = diag_inverse.shape[1]
        self.cores = 2 if self.poles % 2 == 0 else 1
        self.outer = self.poles // self.cores


def swap_sum(part, axis, size, group, stride, held_as):
    at = lax.axis_index(axis)
    digit = (at // stride) % group
    total = lax.dynamic_index_in_dim(part, digit, 0, keepdims=False)
    for step in range(1, group):
        perm = []
        for i in range(size):
            d = (i // stride) % group
            perm.append((i, i + ((d + step) % group - d) * stride))
        to = (digit + step) % group
        send = lax.dynamic_index_in_dim(part, to, 0, keepdims=False).astype(held_as)
        total = total + lax.ppermute(send, axis, perm).astype(F32)
    return total


def generic(sz, green, factor, diag_inverse, pole_weight, pattern):
    block, per_row, cols = sz.block, sz.per_row, sz.width
    row_at = lax.axis_index("row")
    col_at = lax.axis_index("col")
    pattern_f = pattern.astype(F32)
    here = lax.dynamic_slice(pattern_f, (0, col_at * sz.level), (sz.anc, sz.level))
    keep = jnp.repeat(here, block, axis=1)
    own_keep = lax.dynamic_slice_in_dim(keep, row_at * per_row, per_row, 0)
    weight = pole_weight[0]
    gl = green[0]
    fac = factor[0].reshape(per_row, block, cols)
    got = {}
    for shift in range(1, sz.cols):
        perm = [(i, (i + shift) % sz.cols) for i in range(sz.cols)]
        for j in range(sz.half):
            got[shift, j] = lax.ppermute(gl[:, j * block:(j + 1) * block], "col", perm)
    right = [(i, i + 1) for i in range(sz.rows - 1)]
    left = [(i + 1, i) for i in range(sz.rows - 1)]
    blocks = {(0, e): fac[e] for e in range(per_row)}
    from_left, from_right = {}, {}
    for e in range(per_row):
        a = b = fac[e]
        for step in range(1, sz.rows):
            from_left[step, e] = a = lax.ppermute(a, "row", right)
            from_right[step, e] = b = lax.ppermute(b, "row", left)
    for step in range(1, sz.rows):
        for e in range(per_row):
            blocks[step, e] = jnp.where(row_at >= step, from_left[step, e], from_right[sz.rows - step, e])
    stacked = jnp.stack([blocks[s, e] for s in range(sz.rows) for e in range(per_row)])

    def factor_of(a):
        at = ((row_at - a // per_row) % sz.rows) * per_row + a % per_row
        kept = lax.dynamic_index_in_dim(keep, a, 0).astype(BF16)
        return lax.dynamic_index_in_dim(stacked, at, 0, keepdims=False) * kept

    product = jnp.zeros((sz.local_rows, cols), F32)
    for shift in range(sz.cols):
        for j in range(sz.half):
            src = (col_at - shift) % sz.cols
            g = gl[:, j * block:(j + 1) * block] if shift == 0 else got[shift, j]
            product += jnp.dot(g, factor_of(src * sz.half + j), preferred_element_type=F32)
    product = product.reshape(per_row, block, cols) * own_keep[:, None, :]
    update = product.astype(BF16).reshape(sz.local_rows, sz.level, block)
    masked = (fac * own_keep.astype(BF16)[:, None, :]).reshape(sz.local_rows, sz.level, block)
    cross = jnp.einsum("rka,rkb->akb", masked, update, preferred_element_type=F32).reshape(block, cols)
    diag = -weight * cross
    mine = lax.dynamic_slice_in_dim(diag, row_at * sz.count, sz.count, 0)
    mine = mine + weight * diag_inverse[0].astype(F32)
    diag = lax.dynamic_update_slice_in_dim(diag, mine, row_at * sz.count, 0)
    off = -weight * product.reshape(sz.local_rows, cols)
    res = []
    for x in (diag, off):
        r = x.shape[0] // sz.poles
        x = x.reshape(sz.outer, sz.cores, r, cols).transpose(1, 0, 2, 3)
        x = swap_sum(x, "pole", sz.poles, sz.cores, 1, BF16)
        res.append(swap_sum(x, "pole", sz.poles, sz.outer, sz.cores, BF16))
    diag, off = res
    return off, swap_sum(diag.reshape(sz.rows, -1, cols), "row", sz.rows, sz.rows, 1, BF16)


def swap_ranks(sz, pat, row, to):
    base = (1 - to) * sz.half
    need, dist = [], []
    for j in range(sz.half):
        need.append(pat[base + j, to])
        dist.append(jnp.abs((base + j) // sz.per_row - row))
    rank = []
    for j in range(sz.half):
        n = jnp.int32(0)
        for i in range(sz.half):
            if i != j:
                before = dist[i] <= dist[j] if i < j else dist[i] < dist[j]
                n = n + jnp.where(before, need[i], 0)
        rank.append(n)
    return need, rank


def pick_kernel(sz, slot, parts, pos, pat, green, out, buf, in_sem, out_sem):
    need, rank = swap_ranks(sz, pat, pos[1], 1 - pos[2])
    at = jnp.int32(0)
    for j in range(sz.half):
        at = jnp.where(jnp.logical_and(need[j] > 0, rank[j] == slot), j, at)
    at = pl.multiple_of(at * sz.block, sz.block)
    n = sz.local_rows // parts
    ins, outs = [], []
    for i in range(parts):
        ins.append(pltpu.make_async_copy(green.at[0, pl.ds(i * n, n), pl.ds(at, sz.block)], buf.at[i], in_sem.at[i]))
        outs.append(pltpu.make_async_copy(buf.at[i], out.at[pl.ds(i * n, n)], out_sem.at[i]))
        ins[i].start()
    for i in range(parts):
        ins[i].wait()
        outs[i].start()
    for i in range(parts):
        outs[i].wait()


def pick(sz, slot, pos, pattern, green):
    parts = 4
    return pl.pallas_call(
        functools.partial(pick_kernel, sz, slot, parts),
        out_shape=jax.ShapeDtypeStruct((sz.local_rows, sz.block), BF16),
        in_specs=[SMEM, SMEM, ANY],
        out_specs=ANY,
        scratch_shapes=[
            pltpu.VMEM((parts, sz.local_rows // parts, sz.block), BF16),
            pltpu.SemaphoreType.DMA((parts,)),
            pltpu.SemaphoreType.DMA((parts,)),
        ],
    )(pos, pattern, green)


def product_jobs(sz, pos, pat, ready, before, m_refs, g_local, g_slots, job, bufs, total):
    m_buf, g_buf, m_sem, g_sem = bufs
    row, col = pos[1], pos[2]
    _, rank = swap_ranks(sz, pat, row, col)

    def inside(bound, dist, e, slot):
        if bound is None:
            return jnp.bool_(False)
        d, last_e, s = bound
        near = jnp.logical_or(dist < d, jnp.logical_and(dist == d, e <= last_e))
        return jnp.logical_and(near, slot <= s)

    count = jnp.int32(0)
    for a in range(sz.anc):
        away = a // sz.per_row - row
        dist, e = jnp.abs(away), a % sz.per_row
        local = (a // sz.half) == col
        slot = jnp.where(local, -1, rank[a % sz.half])
        todo = jnp.logical_and(inside(ready, dist, e, slot), jnp.logical_not(inside(before, dist, e, slot)))
        todo = jnp.logical_and(todo, pat[a, col] > 0)

        @pl.when(todo)
        def _(a=a, count=count, slot=slot, away=away):
            job[0, count] = away * sz.per_row + a % sz.per_row
            job[1, count] = slot
            job[2, count] = a % sz.half

        count = count + jnp.where(todo, 1, 0)

    def fetch(n, into):
        for key, ref in m_refs.items():
            @pl.when(job[0, n] == key)
            def _(ref=ref):
                pltpu.make_async_copy(ref, m_buf.at[into], m_sem.at[into]).start()

        @pl.when(job[1, n] < 0)
        def _():
            at = pl.multiple_of(job[2, n] * sz.block, sz.block)
            pltpu.make_async_copy(g_local.at[0, :, pl.ds(at, sz.block)], g_buf.at[into], g_sem.at[into]).start()

        for s, ref in enumerate(g_slots):
            @pl.when(job[1, n] == s)
            def _(ref=ref):
                pltpu.make_async_copy(ref, g_buf.at[into], g_sem.at[into]).start()

    @pl.when(count > 0)
    def _():
        fetch(0, 0)

    def step(n, carry):
        now = lax.rem(n, 2)

        @pl.when(n + 1 < count)
        def _():
            fetch(n + 1, 1 - now)

        pltpu.make_async_copy(m_buf.at[now], m_buf.at[now], m_sem.at[now]).wait()
        pltpu.make_async_copy(g_buf.at[now], g_buf.at[now], g_sem.at[now]).wait()
        total[...] += jnp.dot(g_buf[now], m_buf[now], preferred_element_type=F32)
        return carry

    lax.fori_loop(0, count, step, 0)


def job_scratch(sz):
    return [
        pltpu.SMEM((3, sz.anc), jnp.int32),
        pltpu.VMEM((2, sz.block, sz.width), BF16),
        pltpu.VMEM((2, sz.local_rows, sz.block), BF16),
        pltpu.SemaphoreType.DMA((2,)),
        pltpu.SemaphoreType.DMA((2,)),
    ]


def early_kernel(sz, ready, before, keys, n_slots, first, pos, pat, g_local, *refs):
    refs = list(refs)
    m_refs = {k: refs.pop(0) for k in keys}
    g_slots = [refs.pop(0) for _ in range(n_slots)]
    total_in = None if first else refs.pop(0)
    out = refs.pop(0)
    job, m_buf, g_buf, m_sem, g_sem = refs
    if first:
        out[...] = jnp.zeros_like(out)
    else:
        out[...] = total_in[...]
    product_jobs(sz, pos, pat, ready, before, m_refs, g_local, g_slots, job, (m_buf, g_buf, m_sem, g_sem), out)


def early(sz, ready, before, pos, pattern, green, m, slots, total):
    keys = list(m)
    first = total is None
    args = [pos, pattern, green] + [m[k] for k in keys] + list(slots) + ([] if first else [total])
    return early_call(sz, ready, before, keys, slots, first, args)


def early_call(sz, ready, before, keys, slots, first, args):
    return pl.pallas_call(
        functools.partial(early_kernel, sz, ready, before, keys, len(slots), first),
        out_shape=jax.ShapeDtypeStruct((sz.local_rows, sz.width), F32),
        in_specs=[SMEM, SMEM] + [ANY] * (1 + len(keys) + len(slots)) + ([] if first else [VMEM]),
        out_specs=VMEM,
        scratch_shapes=job_scratch(sz),
        input_output_aliases={} if first else {len(args) - 1: 0},
    )(*args)


def pole_steps(sz):
    return [(dx, dc) for dx in range(sz.outer) for dc in range(sz.cores) if dx or dc]


def pole_perm(sz, step):
    dx, dc = step
    return [(x * sz.cores + c, (x + dx) % sz.outer * sz.cores + (c + dc) % sz.cores)
            for x in range(sz.outer) for c in range(sz.cores)]


def late_kernel(sz, ready, before, keys, n_slots, pos, pat, weight, g_local, *refs):
    refs = list(refs)
    m_refs = {k: refs.pop(0) for k in keys}
    g_slots = [refs.pop(0) for _ in range(n_slots)]
    total_in, factor, dinv = refs.pop(0), refs.pop(0), refs.pop(0)
    diag_out = [refs.pop(0) for _ in range(sz.poles)]
    off_out = [refs.pop(0) for _ in range(sz.poles)]
    total, diag = refs.pop(0), refs.pop(0)
    job, m_buf, g_buf, m_sem, g_sem = refs
    row, col = pos[1], pos[2]
    core, x_at = lax.rem(pos[0], sz.cores), pos[0] // sz.cores
    total[...] = total_in[...]
    product_jobs(sz, pos, pat, ready, before, m_refs, g_local, g_slots, job, (m_buf, g_buf, m_sem, g_sem), total)
    w = weight[0]
    diag[...] = jnp.zeros_like(diag)
    for e in range(sz.per_row):
        at = pl.ds(e * sz.block, sz.block)
        kept = pat[row * sz.per_row + e, col] > 0

        @pl.when(kept)
        def _(at=at):
            update = total[at, :]
            diag[...] -= w * lax.dot_general(
                factor[0, at, :], update.astype(BF16), (((0,), (0,)), ((), ())), preferred_element_type=F32)
            total[at, :] = -w * update

        @pl.when(jnp.logical_not(kept))
        def _(at=at):
            total[at, :] = jnp.zeros((sz.block, sz.width), F32)
    mine = pl.ds(pl.multiple_of(row * sz.count, sz.count), sz.count)
    diag[mine, :] += w * dinv[0].astype(F32)
    for src, keep, sends in ((diag, diag_out[0], diag_out[1:]), (total, off_out[0], off_out[1:])):
        n = src.shape[0] // sz.poles

        def part(x, c):
            return src[pl.ds(pl.multiple_of((x * sz.cores + c) * n, n), n), :]

        keep[...] = part(x_at, core)
        for (dx, dc), send in zip(pole_steps(sz), sends):
            send[...] = part(lax.rem(x_at + dx, sz.outer), lax.rem(core + dc, sz.cores)).astype(BF16)


def late(sz, ready, before, pos, pattern, weight, green, m, slots, total, factor, dinv):
    keys = list(m)
    args = [pos, pattern, weight, green] + [m[k] for k in keys] + list(slots) + [total, factor, dinv]
    shapes = []
    for n in (sz.block, sz.local_rows):
        for i in range(sz.poles):
            shapes.append(jax.ShapeDtypeStruct((n // sz.poles, sz.width), BF16 if i else F32))
    return pl.pallas_call(
        functools.partial(late_kernel, sz, ready, before, keys, len(slots)),
        out_shape=shapes,
        in_specs=[SMEM] * 3 + [ANY] * (1 + len(keys) + len(slots)) + [VMEM] * 3,
        out_specs=[VMEM] * (2 * sz.poles),
        scratch_shapes=[pltpu.VMEM((sz.local_rows, sz.width), F32), pltpu.VMEM((sz.block, sz.width), F32)]
        + job_scratch(sz),
        name="late",
    )(*args)


def fold_kernel(group, n_in, axis_pos, stride, pos, keep, *refs):
    ins, outs = refs[:n_in], refs[n_in:]
    own, sends = outs[0], outs[1:]
    n = own.shape[0]
    me = lax.rem(pos[axis_pos] // stride, group)

    def part(d):
        at = pl.ds(pl.multiple_of(d * n, n), n)
        v = keep[at, :]
        for r in ins:
            v = v + r[at, :].astype(F32)
        return v

    for s, send in enumerate(sends):
        send[...] = part(lax.rem(me + s + 1, group)).astype(BF16)
    own[...] = part(me)


def fold(group, axis_pos, stride, pos, keep, ins):
    n, width = keep.shape[0] // group, keep.shape[1]
    shapes = [jax.ShapeDtypeStruct((n, width), F32)] + [jax.ShapeDtypeStruct((n, width), BF16)] * (group - 1)
    return pl.pallas_call(
        functools.partial(fold_kernel, group, len(ins), axis_pos, stride),
        out_shape=shapes,
        in_specs=[SMEM] + [VMEM] * (1 + len(ins)),
        out_specs=[VMEM] * group,
    )(pos, keep, *ins)


def shifts(size, group, stride):
    perms = []
    for step in range(1, group):
        perm = []
        for i in range(size):
            d = (i // stride) % group
            perm.append((i, i + ((d + step) % group - d) * stride))
        perms.append(perm)
    return perms


def blocked(sz, green, factor, diag_inverse, pole_weight, pattern):
    block, per_row = sz.block, sz.per_row
    pos = jnp.stack([lax.axis_index(a) for a in ("pole", "row", "col")]).astype(jnp.int32)
    fac = [factor[0, e * block:(e + 1) * block] for e in range(per_row)]
    right = [(i, i + 1) for i in range(sz.rows - 1)]
    left = [(i + 1, i) for i in range(sz.rows - 1)]
    swap = [(0, 1), (1, 0)]

    fixed = max(sz.half - 1, 1)
    slots = []
    for s in range(fixed):
        sent = pick(sz, s, pos, pattern, green)
        slots.append(lax.ppermute(sent, "col", swap))

    m = {e: fac[e] for e in range(per_row)}
    for e in range(per_row):
        a = b = fac[e]
        for step in range(1, sz.rows):
            m[-step * per_row + e] = a = lax.ppermute(a, "row", right)
            m[step * per_row + e] = b = lax.ppermute(b, "row", left)

    def upto(dist, last_e):
        return {k: v for k, v in m.items() if abs(k // per_row) < dist or (abs(k // per_row) == dist and k % per_row <= last_e)}

    far = sz.rows - 1
    bounds = [(far - 2, per_row - 1, 0), (far - 1, per_row - 1, fixed - 2), (far, per_row - 2, fixed - 2)]

    def part(i, total):
        dist, last_e, s = bounds[i]
        return early(sz, bounds[i], bounds[i - 1] if i else None, pos, pattern, green,
                     upto(dist, last_e), slots[:s + 1], total)

    total = part(1, part(0, None))
    extra = []
    if sz.half > fixed:
        full = jnp.bool_(False)
        for c in range(sz.cols):
            other = (1 - c) * sz.half
            full = jnp.logical_or(full, jnp.all(pattern[other:other + sz.half, c] > 0))

        def more(g):
            return lax.ppermute(pick(sz, fixed, pos, pattern, g), "col", swap)

        full, total = lax.optimization_barrier((full, total))
        got = lax.cond(full, more, lambda g: jnp.zeros((sz.local_rows, block), BF16), green)
        got, total = lax.optimization_barrier((got, total))
        extra.append(got)
    total = part(2, total)
    out = late(sz, (far, per_row - 1, sz.half), bounds[2], pos, pattern, pole_weight, green, m,
               slots + extra, total, factor, diag_inverse)

    def swapped(keep, *sends):
        ins = []
        for v, step in zip(sends, pole_steps(sz)):
            ins.append(lax.ppermute(v, "pole", pole_perm(sz, step)))
        return keep, ins

    diag, diag_in = swapped(*out[:sz.poles])
    off, off_in = swapped(*out[sz.poles:])
    diag, *sends = fold(sz.rows, 1, 1, pos, diag, diag_in)
    diag_in = []
    for v, p in zip(sends, shifts(sz.rows, sz.rows, 1)):
        diag_in.append(lax.ppermute(v, "row", p))
    for v in off_in:
        off = off + v.astype(F32)
    for v in diag_in:
        diag = diag + v.astype(F32)
    return off, diag


def make_body(mesh):
    def body(green, factor, diag_inverse, pole_weight, pattern):
        sz = Sizes(mesh, green, factor, diag_inverse, pattern)
        fits = sz.cols == 2 and sz.level == 1 and sz.cores == 2 and sz.rows >= 3 and sz.per_row >= 2 and sz.half >= 3
        if not fits:
            return generic(sz, green, factor, diag_inverse, pole_weight, pattern)
        return blocked(sz, green, factor, diag_inverse, pole_weight, pattern)

    return body


def solution(mesh):
    in_specs = (
        P("pole", "row", "col"),
        P("pole", "row", "col"),
        P("pole", "row", "col"),
        P("pole"),
        P(),
    )
    out_specs = (P(("row", "pole"), "col"), P(("pole", "row"), "col"))
    return jax.shard_map(make_body(mesh), mesh=mesh, in_specs=in_specs, out_specs=out_specs, check_vma=False)
```

```python
import functools

import jax
import jax.numpy as jnp
from jax import lax
from jax.experimental import pallas as pl
from jax.experimental.pallas import tpu as pltpu
from jax.sharding import PartitionSpec as P


VMEM = pl.BlockSpec(memory_space=pltpu.VMEM)
SMEM = pl.BlockSpec(memory_space=pltpu.SMEM)
ANY = pl.BlockSpec(memory_space=pltpu.HBM)
SMALL = pltpu.CompilerParams(vmem_limit_bytes=12 * 2**20)
F32 = jnp.float32
BF16 = jnp.bfloat16


class Sizes:
    def __init__(self, mesh, green, factor, diag_inverse, pattern):
        self.poles, self.rows, self.cols = (mesh.shape[a] for a in ("pole", "row", "col"))
        self.local_rows, self.k_local = green.shape[1], green.shape[2]
        self.width = factor.shape[2]
        self.anc, supers = pattern.shape
        self.block = self.local_rows * self.rows // self.anc
        self.per_row = self.local_rows // self.block
        self.half = self.k_local // self.block
        self.level = supers // self.cols
        self.count = diag_inverse.shape[1]
        self.cores = 2 if self.poles % 2 == 0 else 1
        self.outer = self.poles // self.cores


def swap_sum(part, axis, size, group, stride, held_as):
    at = lax.axis_index(axis)
    digit = (at // stride) % group
    total = lax.dynamic_index_in_dim(part, digit, 0, keepdims=False)
    for step in range(1, group):
        perm = []
        for i in range(size):
            d = (i // stride) % group
            perm.append((i, i + ((d + step) % group - d) * stride))
        to = (digit + step) % group
        send = lax.dynamic_index_in_dim(part, to, 0, keepdims=False).astype(held_as)
        total = total + lax.ppermute(send, axis, perm).astype(F32)
    return total


def generic(sz, green, factor, diag_inverse, pole_weight, pattern):
    block, per_row, cols = sz.block, sz.per_row, sz.width
    row_at = lax.axis_index("row")
    col_at = lax.axis_index("col")
    pattern_f = pattern.astype(F32)
    here = lax.dynamic_slice(pattern_f, (0, col_at * sz.level), (sz.anc, sz.level))
    keep = jnp.repeat(here, block, axis=1)
    own_keep = lax.dynamic_slice_in_dim(keep, row_at * per_row, per_row, 0)
    weight = pole_weight[0]
    gl = green[0]
    fac = factor[0].reshape(per_row, block, cols)
    got = {}
    for shift in range(1, sz.cols):
        perm = [(i, (i + shift) % sz.cols) for i in range(sz.cols)]
        for j in range(sz.half):
            got[shift, j] = lax.ppermute(gl[:, j * block:(j + 1) * block], "col", perm)
    right = [(i, i + 1) for i in range(sz.rows - 1)]
    left = [(i + 1, i) for i in range(sz.rows - 1)]
    blocks = {(0, e): fac[e] for e in range(per_row)}
    from_left, from_right = {}, {}
    for e in range(per_row):
        a = b = fac[e]
        for step in range(1, sz.rows):
            from_left[step, e] = a = lax.ppermute(a, "row", right)
            from_right[step, e] = b = lax.ppermute(b, "row", left)
    for step in range(1, sz.rows):
        for e in range(per_row):
            blocks[step, e] = jnp.where(row_at >= step, from_left[step, e], from_right[sz.rows - step, e])
    stacked = jnp.stack([blocks[s, e] for s in range(sz.rows) for e in range(per_row)])

    def factor_of(a):
        at = ((row_at - a // per_row) % sz.rows) * per_row + a % per_row
        kept = lax.dynamic_index_in_dim(keep, a, 0).astype(BF16)
        return lax.dynamic_index_in_dim(stacked, at, 0, keepdims=False) * kept

    product = jnp.zeros((sz.local_rows, cols), F32)
    for shift in range(sz.cols):
        for j in range(sz.half):
            src = (col_at - shift) % sz.cols
            g = gl[:, j * block:(j + 1) * block] if shift == 0 else got[shift, j]
            product += jnp.dot(g, factor_of(src * sz.half + j), preferred_element_type=F32)
    product = product.reshape(per_row, block, cols) * own_keep[:, None, :]
    update = product.astype(BF16).reshape(sz.local_rows, sz.level, block)
    masked = (fac * own_keep.astype(BF16)[:, None, :]).reshape(sz.local_rows, sz.level, block)
    cross = jnp.einsum("rka,rkb->akb", masked, update, preferred_element_type=F32).reshape(block, cols)
    diag = -weight * cross
    mine = lax.dynamic_slice_in_dim(diag, row_at * sz.count, sz.count, 0)
    mine = mine + weight * diag_inverse[0].astype(F32)
    diag = lax.dynamic_update_slice_in_dim(diag, mine, row_at * sz.count, 0)
    off = -weight * product.reshape(sz.local_rows, cols)
    res = []
    for x in (diag, off):
        r = x.shape[0] // sz.poles
        x = x.reshape(sz.outer, sz.cores, r, cols).transpose(1, 0, 2, 3)
        x = swap_sum(x, "pole", sz.poles, sz.cores, 1, BF16)
        res.append(swap_sum(x, "pole", sz.poles, sz.outer, sz.cores, BF16))
    diag, off = res
    return off, swap_sum(diag.reshape(sz.rows, -1, cols), "row", sz.rows, sz.rows, 1, BF16)


def swap_ranks(sz, pat, row, to):
    base = (1 - to) * sz.half
    need, dist = [], []
    for j in range(sz.half):
        need.append(pat[to, base + j])
        dist.append(jnp.abs((base + j) // sz.per_row - row))
    rank = []
    for j in range(sz.half):
        n = jnp.int32(0)
        for i in range(sz.half):
            if i != j:
                before = dist[i] <= dist[j] if i < j else dist[i] < dist[j]
                n = n + jnp.where(before, need[i], 0)
        rank.append(n)
    return need, rank


def pick_kernel(sz, slot, parts, pat, green, out, buf, in_sem, out_sem):
    need, rank = swap_ranks(sz, pat, lax.axis_index("row"), 1 - lax.axis_index("col"))
    at = jnp.int32(0)
    for j in range(sz.half):
        at = jnp.where(jnp.logical_and(need[j] > 0, rank[j] == slot), j, at)
    at = pl.multiple_of(at * sz.block, sz.block)
    n = sz.local_rows // parts
    ins, outs = [], []
    for i in range(parts):
        ins.append(pltpu.make_async_copy(green.at[0, pl.ds(i * n, n), pl.ds(at, sz.block)], buf.at[i], in_sem.at[i]))
        outs.append(pltpu.make_async_copy(buf.at[i], out.at[pl.ds(i * n, n)], out_sem.at[i]))
        ins[i].start()
    for i in range(parts):
        ins[i].wait()
        outs[i].start()
    for i in range(parts):
        outs[i].wait()


def pick(sz, slot, pattern, green):
    parts = 4
    return pl.pallas_call(
        functools.partial(pick_kernel, sz, slot, parts),
        out_shape=jax.ShapeDtypeStruct((sz.local_rows, sz.block), BF16),
        in_specs=[SMEM, ANY],
        out_specs=ANY,
        scratch_shapes=[
            pltpu.VMEM((parts, sz.local_rows // parts, sz.block), BF16),
            pltpu.SemaphoreType.DMA((parts,)),
            pltpu.SemaphoreType.DMA((parts,)),
        ],
        compiler_params=SMALL,
    )(pattern, *in_hbm([green]))


def product_jobs(sz, pat, ready, before, m_refs, g_local, g_slots, job, bufs, total):
    m_buf, g_buf, m_sem, g_sem = bufs
    row, col = lax.axis_index("row"), lax.axis_index("col")
    _, rank = swap_ranks(sz, pat, row, col)

    def inside(bound, dist, e, slot):
        if bound is None:
            return jnp.bool_(False)
        d, last_e, s = bound
        near = jnp.logical_or(dist < d, jnp.logical_and(dist == d, e <= last_e))
        return jnp.logical_and(near, slot <= s)

    count = jnp.int32(0)
    for a in range(sz.anc):
        away = a // sz.per_row - row
        dist, e = jnp.abs(away), a % sz.per_row
        local = (a // sz.half) == col
        slot = jnp.where(local, -1, rank[a % sz.half])
        todo = jnp.logical_and(inside(ready, dist, e, slot), jnp.logical_not(inside(before, dist, e, slot)))
        todo = jnp.logical_and(todo, pat[col, a] > 0)

        @pl.when(todo)
        def _(a=a, count=count, slot=slot, away=away):
            job[0, count] = away * sz.per_row + a % sz.per_row
            job[1, count] = slot
            job[2, count] = a % sz.half

        count = count + jnp.where(todo, 1, 0)

    def fetch(n, into):
        for key, ref in m_refs.items():
            @pl.when(job[0, n] == key)
            def _(ref=ref):
                pltpu.make_async_copy(ref, m_buf.at[into], m_sem.at[into]).start()

        @pl.when(job[1, n] < 0)
        def _():
            at = pl.multiple_of(job[2, n] * sz.block, sz.block)
            pltpu.make_async_copy(g_local.at[0, :, pl.ds(at, sz.block)], g_buf.at[into], g_sem.at[into]).start()

        for s, ref in enumerate(g_slots):
            @pl.when(job[1, n] == s)
            def _(ref=ref):
                pltpu.make_async_copy(ref, g_buf.at[into], g_sem.at[into]).start()

    @pl.when(count > 0)
    def _():
        fetch(0, 0)

    def step(n, carry):
        now = lax.rem(n, 2)

        @pl.when(n + 1 < count)
        def _():
            fetch(n + 1, 1 - now)

        pltpu.make_async_copy(m_buf.at[now], m_buf.at[now], m_sem.at[now]).wait()
        pltpu.make_async_copy(g_buf.at[now], g_buf.at[now], g_sem.at[now]).wait()
        total[...] += jnp.dot(g_buf[now], m_buf[now], preferred_element_type=F32)
        return carry

    lax.fori_loop(0, count, step, 0)


def in_hbm(arrays):
    return [pltpu.with_memory_space_constraint(a, pltpu.HBM) for a in arrays]


def job_scratch(sz):
    return [
        pltpu.SMEM((3, sz.anc), jnp.int32),
        pltpu.VMEM((2, sz.block, sz.width), BF16),
        pltpu.VMEM((2, sz.local_rows, sz.block), BF16),
        pltpu.SemaphoreType.DMA((2,)),
        pltpu.SemaphoreType.DMA((2,)),
    ]


def early_kernel(sz, ready, before, keys, n_slots, first, pat, g_local, *refs):
    refs = list(refs)
    m_refs = {k: refs.pop(0) for k in keys}
    g_slots = [refs.pop(0) for _ in range(n_slots)]
    total_in = None if first else refs.pop(0)
    out = refs.pop(0)
    job, m_buf, g_buf, m_sem, g_sem = refs
    if first:
        out[...] = jnp.zeros_like(out)
    else:
        out[...] = total_in[...]
    product_jobs(sz, pat, ready, before, m_refs, g_local, g_slots, job, (m_buf, g_buf, m_sem, g_sem), out)


def early(sz, ready, before, pattern, green, m, slots, total):
    keys = list(m)
    first = total is None
    args = [pattern] + in_hbm([green] + [m[k] for k in keys] + list(slots)) + ([] if first else [total])
    return early_call(sz, ready, before, keys, slots, first, args)


def early_call(sz, ready, before, keys, slots, first, args):
    return pl.pallas_call(
        functools.partial(early_kernel, sz, ready, before, keys, len(slots), first),
        out_shape=jax.ShapeDtypeStruct((sz.local_rows, sz.width), F32),
        in_specs=[SMEM] + [ANY] * (1 + len(keys) + len(slots)) + ([] if first else [VMEM]),
        out_specs=VMEM,
        scratch_shapes=job_scratch(sz),
        input_output_aliases={} if first else {len(args) - 1: 0},
        compiler_params=SMALL,
    )(*args)


def pole_steps(sz):
    return [(dx, dc) for dx in range(sz.outer) for dc in range(sz.cores) if dx or dc]


def pole_perm(sz, step):
    dx, dc = step
    return [(x * sz.cores + c, (x + dx) % sz.outer * sz.cores + (c + dc) % sz.cores)
            for x in range(sz.outer) for c in range(sz.cores)]


def late_kernel(sz, ready, before, keys, n_slots, pat, weight, g_local, *refs):
    refs = list(refs)
    m_refs = {k: refs.pop(0) for k in keys}
    g_slots = [refs.pop(0) for _ in range(n_slots)]
    total_in, factor, dinv = refs.pop(0), refs.pop(0), refs.pop(0)
    diag_out = [refs.pop(0) for _ in range(sz.poles)]
    off_out = [refs.pop(0) for _ in range(sz.cores)]
    total, diag = refs.pop(0), refs.pop(0)
    job, m_buf, g_buf, m_sem, g_sem = refs
    row, col, pole = (lax.axis_index(a) for a in ("row", "col", "pole"))
    core, x_at = lax.rem(pole, sz.cores), pole // sz.cores
    total[...] = total_in[...]
    product_jobs(sz, pat, ready, before, m_refs, g_local, g_slots, job, (m_buf, g_buf, m_sem, g_sem), total)
    w = weight[0]
    diag[...] = jnp.zeros_like(diag)
    for e in range(sz.per_row):
        at = pl.ds(e * sz.block, sz.block)
        kept = pat[col, row * sz.per_row + e] > 0

        @pl.when(kept)
        def _(at=at):
            update = total[at, :]
            diag[...] -= w * lax.dot_general(
                factor[0, at, :], update.astype(BF16), (((0,), (0,)), ((), ())), preferred_element_type=F32)
            total[at, :] = -w * update

        @pl.when(jnp.logical_not(kept))
        def _(at=at):
            total[at, :] = jnp.zeros((sz.block, sz.width), F32)
    mine = pl.ds(pl.multiple_of(row * sz.count, sz.count), sz.count)
    diag[mine, :] += w * dinv[0].astype(F32)
    n = diag.shape[0] // sz.poles
    for (dx, dc), out in zip([(0, 0)] + pole_steps(sz), diag_out):
        q = lax.rem(x_at + dx, sz.outer) * sz.cores + lax.rem(core + dc, sz.cores)
        out[...] = diag[pl.ds(pl.multiple_of(q * n, n), n), :].astype(out.dtype)
    n = total.shape[0] // sz.poles
    for dc, out in enumerate(off_out):
        for x in range(sz.outer):
            q = x * sz.cores + lax.rem(core + dc, sz.cores)
            out[x * n:(x + 1) * n, :] = total[pl.ds(pl.multiple_of(q * n, n), n), :].astype(out.dtype)


def late(sz, ready, before, pattern, weight, green, m, slots, total, factor, dinv):
    keys = list(m)
    args = [pattern, weight] + in_hbm([green] + [m[k] for k in keys] + list(slots)) + [total, factor, dinv]
    shapes = [jax.ShapeDtypeStruct((sz.block // sz.poles, sz.width), BF16 if i else F32) for i in range(sz.poles)]
    shapes += [jax.ShapeDtypeStruct((sz.local_rows // sz.cores, sz.width), BF16 if i else F32) for i in range(sz.cores)]
    return pl.pallas_call(
        functools.partial(late_kernel, sz, ready, before, keys, len(slots)),
        out_shape=shapes,
        in_specs=[SMEM] * 2 + [ANY] * (1 + len(keys) + len(slots)) + [VMEM] * 3,
        out_specs=[VMEM] * (sz.poles + sz.cores),
        scratch_shapes=[pltpu.VMEM((sz.local_rows, sz.width), F32), pltpu.VMEM((sz.block, sz.width), F32)]
        + job_scratch(sz),
        compiler_params=SMALL,
        name="late",
    )(*args)


def fold_kernel(group, n_in, axis, stride, keep, *refs):
    ins, outs = refs[:n_in], refs[n_in:]
    own, sends = outs[0], outs[1:]
    n = own.shape[0]
    me = lax.rem(lax.axis_index(axis) // stride, group)

    def part(d):
        at = pl.ds(pl.multiple_of(d * n, n), n)
        v = keep[at, :]
        for r in ins:
            v = v + r[at, :].astype(F32)
        return v

    for s, send in enumerate(sends):
        send[...] = part(lax.rem(me + s + 1, group)).astype(BF16)
    own[...] = part(me)


def fold(group, axis, stride, keep, ins):
    n, width = keep.shape[0] // group, keep.shape[1]
    shapes = [jax.ShapeDtypeStruct((n, width), F32)] + [jax.ShapeDtypeStruct((n, width), BF16)] * (group - 1)
    return pl.pallas_call(
        functools.partial(fold_kernel, group, len(ins), axis, stride),
        out_shape=shapes,
        in_specs=[VMEM] * (1 + len(ins)),
        out_specs=[VMEM] * group,
        compiler_params=SMALL,
    )(keep, *ins)


def shifts(size, group, stride):
    perms = []
    for step in range(1, group):
        perm = []
        for i in range(size):
            d = (i // stride) % group
            perm.append((i, i + ((d + step) % group - d) * stride))
        perms.append(perm)
    return perms


def blocked(sz, green, factor, diag_inverse, pole_weight, pattern):
    block, per_row = sz.block, sz.per_row
    pattern = pattern.T
    fac = [factor[0, e * block:(e + 1) * block] for e in range(per_row)]
    right = [(i, i + 1) for i in range(sz.rows - 1)]
    left = [(i + 1, i) for i in range(sz.rows - 1)]
    swap = [(0, 1), (1, 0)]

    fixed = max(sz.half - 1, 1)
    slots = []
    for s in range(fixed):
        sent = pick(sz, s, pattern, green)
        slots.append(lax.ppermute(sent, "col", swap))

    m = {e: fac[e] for e in range(per_row)}
    for e in range(per_row):
        a = b = fac[e]
        for step in range(1, sz.rows):
            m[-step * per_row + e] = a = lax.ppermute(a, "row", right)
            m[step * per_row + e] = b = lax.ppermute(b, "row", left)

    def upto(dist, last_e):
        return {k: v for k, v in m.items() if abs(k // per_row) < dist or (abs(k // per_row) == dist and k % per_row <= last_e)}

    far = sz.rows - 1
    bounds = [(far - 2, per_row - 1, 0), (far - 1, per_row - 1, fixed - 2), (far, per_row - 2, fixed - 2)]

    def part(i, total):
        dist, last_e, s = bounds[i]
        return early(sz, bounds[i], bounds[i - 1] if i else None, pattern, green,
                     upto(dist, last_e), slots[:s + 1], total)

    total = part(1, part(0, None))
    extra = []
    if sz.half > fixed:
        full = jnp.bool_(False)
        for c in range(sz.cols):
            other = (1 - c) * sz.half
            full = jnp.logical_or(full, jnp.all(pattern[c, other:other + sz.half] > 0))

        def more(g):
            return lax.ppermute(pick(sz, fixed, pattern, g), "col", swap)

        full, total = lax.optimization_barrier((full, total))
        got = lax.cond(full, more, lambda g: jnp.zeros((sz.local_rows, block), BF16), green)
        got, total = lax.optimization_barrier((got, total))
        extra.append(got)
    total = part(2, total)
    out = late(sz, (far, per_row - 1, sz.half), bounds[2], pattern, pole_weight, green, m,
               slots + extra, total, factor, diag_inverse)

    def swapped(axis, sends, perms):
        ins = []
        for v, perm in zip(sends, perms):
            ins.append(lax.ppermute(v, axis, perm))
        return ins

    diag, *sends = out[:sz.poles]
    diag_in = swapped("pole", sends, [pole_perm(sz, step) for step in pole_steps(sz)])
    off, *sends = out[sz.poles:]
    off_in = swapped("pole", sends, shifts(sz.poles, sz.cores, 1))
    off, *sends = fold(sz.outer, "pole", sz.cores, off, off_in)
    off_in = swapped("pole", sends, shifts(sz.poles, sz.outer, sz.cores))
    diag, *sends = fold(sz.rows, "row", 1, diag, diag_in)
    diag_in = swapped("row", sends, shifts(sz.rows, sz.rows, 1))
    for v in off_in:
        off = off + v.astype(F32)
    for v in diag_in:
        diag = diag + v.astype(F32)
    return off, diag


def make_body(mesh):
    def body(green, factor, diag_inverse, pole_weight, pattern):
        sz = Sizes(mesh, green, factor, diag_inverse, pattern)
        fits = sz.cols == 2 and sz.level == 1 and sz.cores == 2 and sz.rows >= 3 and sz.per_row >= 2 and sz.half >= 3
        if not fits:
            return generic(sz, green, factor, diag_inverse, pole_weight, pattern)
        return blocked(sz, green, factor, diag_inverse, pole_weight, pattern)

    return body


def solution(mesh):
    in_specs = (
        P("pole", "row", "col"),
        P("pole", "row", "col"),
        P("pole", "row", "col"),
        P("pole"),
        P(),
    )
    out_specs = (P(("row", "pole"), "col"), P(("pole", "row"), "col"))
    return jax.shard_map(make_body(mesh), mesh=mesh, in_specs=in_specs, out_specs=out_specs, check_vma=False)
```

```python
import functools

import jax
import jax.numpy as jnp
from jax import lax
from jax.experimental import pallas as pl
from jax.experimental.pallas import tpu as pltpu
from jax.sharding import PartitionSpec as P


VMEM = pl.BlockSpec(memory_space=pltpu.VMEM)
SMEM = pl.BlockSpec(memory_space=pltpu.SMEM)
ANY = pl.BlockSpec(memory_space=pltpu.HBM)
SMALL = pltpu.CompilerParams(vmem_limit_bytes=12 * 2**20)
F32 = jnp.float32
BF16 = jnp.bfloat16


class Sizes:
    def __init__(self, mesh, green, factor, diag_inverse, pattern):
        self.poles, self.rows, self.cols = (mesh.shape[a] for a in ("pole", "row", "col"))
        self.local_rows, self.k_local = green.shape[1], green.shape[2]
        self.width = factor.shape[2]
        self.anc, supers = pattern.shape
        self.block = self.local_rows * self.rows // self.anc
        self.per_row = self.local_rows // self.block
        self.half = self.k_local // self.block
        self.level = supers // self.cols
        self.count = diag_inverse.shape[1]
        self.cores = 2 if self.poles % 2 == 0 else 1
        self.outer = self.poles // self.cores


def swap_sum(part, axis, size, group, stride, held_as):
    at = lax.axis_index(axis)
    digit = (at // stride) % group
    total = lax.dynamic_index_in_dim(part, digit, 0, keepdims=False)
    for step in range(1, group):
        perm = []
        for i in range(size):
            d = (i // stride) % group
            perm.append((i, i + ((d + step) % group - d) * stride))
        to = (digit + step) % group
        send = lax.dynamic_index_in_dim(part, to, 0, keepdims=False).astype(held_as)
        total = total + lax.ppermute(send, axis, perm).astype(F32)
    return total


def generic(sz, green, factor, diag_inverse, pole_weight, pattern):
    block, per_row, cols = sz.block, sz.per_row, sz.width
    row_at = lax.axis_index("row")
    col_at = lax.axis_index("col")
    pattern_f = pattern.astype(F32)
    here = lax.dynamic_slice(pattern_f, (0, col_at * sz.level), (sz.anc, sz.level))
    keep = jnp.repeat(here, block, axis=1)
    own_keep = lax.dynamic_slice_in_dim(keep, row_at * per_row, per_row, 0)
    weight = pole_weight[0]
    gl = green[0]
    fac = factor[0].reshape(per_row, block, cols)
    got = {}
    for shift in range(1, sz.cols):
        perm = [(i, (i + shift) % sz.cols) for i in range(sz.cols)]
        for j in range(sz.half):
            got[shift, j] = lax.ppermute(gl[:, j * block:(j + 1) * block], "col", perm)
    right = [(i, i + 1) for i in range(sz.rows - 1)]
    left = [(i + 1, i) for i in range(sz.rows - 1)]
    blocks = {(0, e): fac[e] for e in range(per_row)}
    from_left, from_right = {}, {}
    for e in range(per_row):
        a = b = fac[e]
        for step in range(1, sz.rows):
            from_left[step, e] = a = lax.ppermute(a, "row", right)
            from_right[step, e] = b = lax.ppermute(b, "row", left)
    for step in range(1, sz.rows):
        for e in range(per_row):
            blocks[step, e] = jnp.where(row_at >= step, from_left[step, e], from_right[sz.rows - step, e])
    stacked = jnp.stack([blocks[s, e] for s in range(sz.rows) for e in range(per_row)])

    def factor_of(a):
        at = ((row_at - a // per_row) % sz.rows) * per_row + a % per_row
        kept = lax.dynamic_index_in_dim(keep, a, 0).astype(BF16)
        return lax.dynamic_index_in_dim(stacked, at, 0, keepdims=False) * kept

    product = jnp.zeros((sz.local_rows, cols), F32)
    for shift in range(sz.cols):
        for j in range(sz.half):
            src = (col_at - shift) % sz.cols
            g = gl[:, j * block:(j + 1) * block] if shift == 0 else got[shift, j]
            product += jnp.dot(g, factor_of(src * sz.half + j), preferred_element_type=F32)
    product = product.reshape(per_row, block, cols) * own_keep[:, None, :]
    update = product.astype(BF16).reshape(sz.local_rows, sz.level, block)
    masked = (fac * own_keep.astype(BF16)[:, None, :]).reshape(sz.local_rows, sz.level, block)
    cross = jnp.einsum("rka,rkb->akb", masked, update, preferred_element_type=F32).reshape(block, cols)
    diag = -weight * cross
    mine = lax.dynamic_slice_in_dim(diag, row_at * sz.count, sz.count, 0)
    mine = mine + weight * diag_inverse[0].astype(F32)
    diag = lax.dynamic_update_slice_in_dim(diag, mine, row_at * sz.count, 0)
    off = -weight * product.reshape(sz.local_rows, cols)
    res = []
    for x in (diag, off):
        r = x.shape[0] // sz.poles
        x = x.reshape(sz.outer, sz.cores, r, cols).transpose(1, 0, 2, 3)
        x = swap_sum(x, "pole", sz.poles, sz.cores, 1, BF16)
        res.append(swap_sum(x, "pole", sz.poles, sz.outer, sz.cores, BF16))
    diag, off = res
    return off, swap_sum(diag.reshape(sz.rows, -1, cols), "row", sz.rows, sz.rows, 1, BF16)


def swap_ranks(sz, pat, row, to):
    base = (1 - to) * sz.half
    need, dist = [], []
    for j in range(sz.half):
        need.append(pat[to, base + j])
        dist.append(jnp.abs((base + j) // sz.per_row - row))
    rank = []
    for j in range(sz.half):
        n = jnp.int32(0)
        for i in range(sz.half):
            if i != j:
                before = dist[i] > dist[j] if i < j else dist[i] >= dist[j]
                n = n + jnp.where(before, need[i], 0)
        rank.append(n)
    return need, rank


def pick_kernel(sz, slot, parts, pat, green, out, buf, in_sem, out_sem):
    need, rank = swap_ranks(sz, pat, lax.axis_index("row"), 1 - lax.axis_index("col"))
    at = jnp.int32(0)
    for j in range(sz.half):
        at = jnp.where(jnp.logical_and(need[j] > 0, rank[j] == slot), j, at)
    at = pl.multiple_of(at * sz.block, sz.block)
    n = sz.local_rows // parts
    ins, outs = [], []
    for i in range(parts):
        ins.append(pltpu.make_async_copy(green.at[0, pl.ds(i * n, n), pl.ds(at, sz.block)], buf.at[i], in_sem.at[i]))
        outs.append(pltpu.make_async_copy(buf.at[i], out.at[pl.ds(i * n, n)], out_sem.at[i]))
        ins[i].start()
    for i in range(parts):
        ins[i].wait()
        outs[i].start()
    for i in range(parts):
        outs[i].wait()


def pick(sz, slot, pattern, green):
    parts = 4
    return pl.pallas_call(
        functools.partial(pick_kernel, sz, slot, parts),
        out_shape=jax.ShapeDtypeStruct((sz.local_rows, sz.block), BF16),
        in_specs=[SMEM, ANY],
        out_specs=ANY,
        scratch_shapes=[
            pltpu.VMEM((parts, sz.local_rows // parts, sz.block), BF16),
            pltpu.SemaphoreType.DMA((parts,)),
            pltpu.SemaphoreType.DMA((parts,)),
        ],
        compiler_params=SMALL,
    )(pattern, *in_hbm([green]))


def product_jobs(sz, pat, ready, before, m_refs, g_local, g_slots, job, bufs, total):
    m_buf, g_buf, m_sem, g_sem = bufs
    row, col = lax.axis_index("row"), lax.axis_index("col")
    _, rank = swap_ranks(sz, pat, row, col)

    def inside(bound, dist, e, slot):
        if bound is None:
            return jnp.bool_(False)
        d, last_e, s = bound
        near = jnp.logical_or(dist < d, jnp.logical_and(dist == d, e <= last_e))
        return jnp.logical_and(near, slot <= s)

    count = jnp.int32(0)
    for a in range(sz.anc):
        away = a // sz.per_row - row
        dist, e = jnp.abs(away), a % sz.per_row
        local = (a // sz.half) == col
        slot = jnp.where(local, -1, rank[a % sz.half])
        todo = jnp.logical_and(inside(ready, dist, e, slot), jnp.logical_not(inside(before, dist, e, slot)))
        todo = jnp.logical_and(todo, pat[col, a] > 0)

        @pl.when(todo)
        def _(a=a, count=count, slot=slot, away=away):
            job[0, count] = away * sz.per_row + a % sz.per_row
            job[1, count] = slot
            job[2, count] = a % sz.half

        count = count + jnp.where(todo, 1, 0)

    def fetch(n, into):
        for key, ref in m_refs.items():
            @pl.when(job[0, n] == key)
            def _(ref=ref):
                pltpu.make_async_copy(ref, m_buf.at[into], m_sem.at[into]).start()

        @pl.when(job[1, n] < 0)
        def _():
            at = pl.multiple_of(job[2, n] * sz.block, sz.block)
            pltpu.make_async_copy(g_local.at[0, :, pl.ds(at, sz.block)], g_buf.at[into], g_sem.at[into]).start()

        for s, ref in enumerate(g_slots):
            @pl.when(job[1, n] == s)
            def _(ref=ref):
                pltpu.make_async_copy(ref, g_buf.at[into], g_sem.at[into]).start()

    @pl.when(count > 0)
    def _():
        fetch(0, 0)

    def step(n, carry):
        now = lax.rem(n, 2)

        @pl.when(n + 1 < count)
        def _():
            fetch(n + 1, 1 - now)

        pltpu.make_async_copy(m_buf.at[now], m_buf.at[now], m_sem.at[now]).wait()
        pltpu.make_async_copy(g_buf.at[now], g_buf.at[now], g_sem.at[now]).wait()
        total[...] += jnp.dot(g_buf[now], m_buf[now], preferred_element_type=F32)
        return carry

    lax.fori_loop(0, count, step, 0)


def in_hbm(arrays):
    return [pltpu.with_memory_space_constraint(a, pltpu.HBM) for a in arrays]


def job_scratch(sz):
    return [
        pltpu.SMEM((3, sz.anc), jnp.int32),
        pltpu.VMEM((2, sz.block, sz.width), BF16),
        pltpu.VMEM((2, sz.local_rows, sz.block), BF16),
        pltpu.SemaphoreType.DMA((2,)),
        pltpu.SemaphoreType.DMA((2,)),
    ]


def early_kernel(sz, ready, before, keys, n_slots, first, pat, g_local, *refs):
    refs = list(refs)
    m_refs = {k: refs.pop(0) for k in keys}
    g_slots = [refs.pop(0) for _ in range(n_slots)]
    total_in = None if first else refs.pop(0)
    out = refs.pop(0)
    job, m_buf, g_buf, m_sem, g_sem = refs
    if first:
        out[...] = jnp.zeros_like(out)
    else:
        out[...] = total_in[...]
    product_jobs(sz, pat, ready, before, m_refs, g_local, g_slots, job, (m_buf, g_buf, m_sem, g_sem), out)


def early(sz, ready, before, pattern, green, m, slots, total):
    keys = list(m)
    first = total is None
    args = [pattern] + in_hbm([green] + [m[k] for k in keys] + list(slots)) + ([] if first else [total])
    return early_call(sz, ready, before, keys, slots, first, args)


def early_call(sz, ready, before, keys, slots, first, args):
    return pl.pallas_call(
        functools.partial(early_kernel, sz, ready, before, keys, len(slots), first),
        out_shape=jax.ShapeDtypeStruct((sz.local_rows, sz.width), F32),
        in_specs=[SMEM] + [ANY] * (1 + len(keys) + len(slots)) + ([] if first else [VMEM]),
        out_specs=VMEM,
        scratch_shapes=job_scratch(sz),
        input_output_aliases={} if first else {len(args) - 1: 0},
        compiler_params=SMALL,
    )(*args)


def pole_steps(sz):
    return [(dx, dc) for dx in range(sz.outer) for dc in range(sz.cores) if dx or dc]


def pole_perm(sz, step):
    dx, dc = step
    return [(x * sz.cores + c, (x + dx) % sz.outer * sz.cores + (c + dc) % sz.cores)
            for x in range(sz.outer) for c in range(sz.cores)]


def far_block(sz, row):
    far = jnp.where(row < sz.rows // 2, sz.rows - 1, 0)
    return far * sz.per_row + sz.per_row - 1


def inner_kernel(sz, pat, green, slot, factor, out, g_buf, sem):
    row, col = lax.axis_index("row"), lax.axis_index("col")
    a = far_block(sz, row)

    @pl.when(a // sz.half == col)
    def _():
        at = pl.multiple_of(lax.rem(a, sz.half) * sz.block, sz.block)
        pltpu.make_async_copy(green.at[0, :, pl.ds(at, sz.block)], g_buf, sem).start()

    @pl.when(a // sz.half != col)
    def _():
        pltpu.make_async_copy(slot, g_buf, sem).start()

    pltpu.make_async_copy(g_buf, g_buf, sem).wait()
    total = jnp.zeros((sz.width, sz.block), F32)
    for e in range(sz.per_row):
        at = pl.ds(e * sz.block, sz.block)
        kept = pat[col, row * sz.per_row + e] > 0
        part = lax.dot_general(factor[0, at, :], g_buf[at, :], (((0,), (0,)), ((), ())), preferred_element_type=F32)
        total = total + jnp.where(kept, part, 0.0)
    out[...] = total.astype(BF16)


def inner(sz, pattern, green, slot, factor):
    return pl.pallas_call(
        functools.partial(inner_kernel, sz),
        out_shape=jax.ShapeDtypeStruct((sz.width, sz.block), BF16),
        in_specs=[SMEM, ANY, ANY, VMEM],
        out_specs=VMEM,
        scratch_shapes=[pltpu.VMEM((sz.local_rows, sz.block), BF16), pltpu.SemaphoreType.DMA],
        compiler_params=SMALL,
        name="inner",
    )(pattern, *in_hbm([green, slot]), factor)


def late_diag_kernel(sz, ready, before, keys, n_slots, pat, weight, g_local, *refs):
    refs = list(refs)
    m_refs = {k: refs.pop(0) for k in keys}
    g_slots = [refs.pop(0) for _ in range(n_slots)]
    total_in, factor, dinv, far_term = (refs.pop(0) for _ in range(4))
    outs = [refs.pop(0) for _ in range(sz.poles)]
    total, diag = refs.pop(0), refs.pop(0)
    job, m_buf, g_buf, m_sem, g_sem = refs
    row, col, pole = (lax.axis_index(a) for a in ("row", "col", "pole"))
    core, x_at = lax.rem(pole, sz.cores), pole // sz.cores

    away = sz.rows - 2
    for at_row, sign in ((1, 1), (sz.rows - 2, -1)):
        key = sign * away * sz.per_row + sz.per_row - 1

        @pl.when(row == at_row)
        def _(key=key):
            copy = pltpu.make_async_copy(m_refs[key], m_buf.at[0], m_sem.at[0])
            copy.start()
            copy.wait()

    inward = jnp.logical_or(row == 1, row == sz.rows - 2)
    a = far_block(sz, row)
    w = weight[0]
    diag[...] = jnp.zeros_like(diag)

    @pl.when(jnp.logical_and(inward, pat[col, a] > 0))
    def _():
        diag[...] -= w * jnp.dot(far_term[...], m_buf[0], preferred_element_type=F32)

    total[...] = total_in[...]
    product_jobs(sz, pat, ready, before, m_refs, g_local, g_slots, job, (m_buf, g_buf, m_sem, g_sem), total)
    for e in range(sz.per_row):
        at = pl.ds(e * sz.block, sz.block)

        @pl.when(pat[col, row * sz.per_row + e] > 0)
        def _(at=at):
            diag[...] -= w * lax.dot_general(
                factor[0, at, :], total[at, :].astype(BF16), (((0,), (0,)), ((), ())), preferred_element_type=F32)

    mine = pl.ds(pl.multiple_of(row * sz.count, sz.count), sz.count)
    diag[mine, :] += w * dinv[0].astype(F32)
    n = diag.shape[0] // sz.poles
    for (dx, dc), out in zip([(0, 0)] + pole_steps(sz), outs):
        q = lax.rem(x_at + dx, sz.outer) * sz.cores + lax.rem(core + dc, sz.cores)
        out[...] = diag[pl.ds(pl.multiple_of(q * n, n), n), :].astype(out.dtype)


def late_diag(sz, ready, before, pattern, weight, green, m, slots, total, factor, dinv, far_term):
    keys = list(m)
    args = [pattern, weight] + in_hbm([green] + [m[k] for k in keys] + list(slots)) + [total, factor, dinv, far_term]
    shapes = [jax.ShapeDtypeStruct((sz.block // sz.poles, sz.width), BF16 if i else F32) for i in range(sz.poles)]
    shapes.append(jax.ShapeDtypeStruct((sz.local_rows, sz.width), F32))
    return pl.pallas_call(
        functools.partial(late_diag_kernel, sz, ready, before, keys, len(slots)),
        out_shape=shapes,
        in_specs=[SMEM] * 2 + [ANY] * (1 + len(keys) + len(slots)) + [VMEM] * 4,
        out_specs=[VMEM] * (sz.poles + 1),
        scratch_shapes=[pltpu.VMEM((sz.block, sz.width), F32)] + job_scratch(sz),
        compiler_params=SMALL,
        name="late_diag",
    )(*args)


def late_off_kernel(sz, ready, before, keys, n_slots, pat, weight, g_local, *refs):
    refs = list(refs)
    m_refs = {k: refs.pop(0) for k in keys}
    g_slots = [refs.pop(0) for _ in range(n_slots)]
    total_in = refs.pop(0)
    outs = [refs.pop(0) for _ in range(sz.cores)]
    total = refs.pop(0)
    job, m_buf, g_buf, m_sem, g_sem = refs
    row, col = lax.axis_index("row"), lax.axis_index("col")
    core = lax.rem(lax.axis_index("pole"), sz.cores)
    total[...] = total_in[...]
    product_jobs(sz, pat, ready, before, m_refs, g_local, g_slots, job, (m_buf, g_buf, m_sem, g_sem), total)
    w = weight[0]
    n = total.shape[0] // sz.poles
    for dc, out in enumerate(outs):
        for x in range(sz.outer):
            q = x * sz.cores + lax.rem(core + dc, sz.cores)
            kept = pat[col, row * sz.per_row + (q * n) // sz.block] > 0
            v = total[pl.ds(pl.multiple_of(q * n, n), n), :]
            out[x * n:(x + 1) * n, :] = jnp.where(kept, -w * v, 0.0).astype(out.dtype)


def late_off(sz, ready, before, pattern, weight, green, m, slots, total):
    keys = list(m)
    args = [pattern, weight] + in_hbm([green] + [m[k] for k in keys] + list(slots)) + [total]
    shapes = [jax.ShapeDtypeStruct((sz.local_rows // sz.cores, sz.width), BF16 if i else F32) for i in range(sz.cores)]
    return pl.pallas_call(
        functools.partial(late_off_kernel, sz, ready, before, keys, len(slots)),
        out_shape=shapes,
        in_specs=[SMEM] * 2 + [ANY] * (1 + len(keys) + len(slots)) + [VMEM],
        out_specs=[VMEM] * sz.cores,
        scratch_shapes=[pltpu.VMEM((sz.local_rows, sz.width), F32)] + job_scratch(sz),
        compiler_params=SMALL,
        name="late_off",
    )(*args)


def fold_kernel(group, n_in, axis, stride, keep, *refs):
    ins, outs = refs[:n_in], refs[n_in:]
    own, sends = outs[0], outs[1:]
    n = own.shape[0]
    me = lax.rem(lax.axis_index(axis) // stride, group)

    def part(d):
        at = pl.ds(pl.multiple_of(d * n, n), n)
        v = keep[at, :]
        for r in ins:
            v = v + r[at, :].astype(F32)
        return v

    for s, send in enumerate(sends):
        send[...] = part(lax.rem(me + s + 1, group)).astype(BF16)
    own[...] = part(me)


def fold(group, axis, stride, keep, ins):
    n, width = keep.shape[0] // group, keep.shape[1]
    shapes = [jax.ShapeDtypeStruct((n, width), F32)] + [jax.ShapeDtypeStruct((n, width), BF16)] * (group - 1)
    return pl.pallas_call(
        functools.partial(fold_kernel, group, len(ins), axis, stride),
        out_shape=shapes,
        in_specs=[VMEM] * (1 + len(ins)),
        out_specs=[VMEM] * group,
        compiler_params=SMALL,
    )(keep, *ins)


def shifts(size, group, stride):
    perms = []
    for step in range(1, group):
        perm = []
        for i in range(size):
            d = (i // stride) % group
            perm.append((i, i + ((d + step) % group - d) * stride))
        perms.append(perm)
    return perms


def blocked(sz, green, factor, diag_inverse, pole_weight, pattern):
    block, per_row = sz.block, sz.per_row
    pattern = pattern.T
    fac = [factor[0, e * block:(e + 1) * block] for e in range(per_row)]
    swap = [(0, 1), (1, 0)]

    fixed = max(sz.half - 1, 1)
    slots = []
    for s in range(fixed):
        sent = pick(sz, s, pattern, green)
        slots.append(lax.ppermute(sent, "col", swap))

    m = {e: fac[e] for e in range(per_row)}
    for e in range(per_row):
        a = b = fac[e]
        for step in range(1, sz.rows):
            m[-step * per_row + e] = a = lax.ppermute(a, "row", [(i, i + 1) for i in range(step - 1, sz.rows - 1)])
            m[step * per_row + e] = b = lax.ppermute(b, "row", [(i + 1, i) for i in range(sz.rows - step)])

    def upto(dist, last_e):
        return {k: v for k, v in m.items() if abs(k // per_row) < dist or (abs(k // per_row) == dist and k % per_row <= last_e)}

    far = sz.rows - 1
    bounds = [(far - 1, per_row - 1, fixed - 2), (far, per_row - 2, fixed - 2)]
    far_term = inner(sz, pattern, green, slots[0], factor)
    far_term = lax.ppermute(far_term, "row", [(0, 1), (far, far - 1)])

    def part(i, total):
        dist, last_e, s = bounds[i]
        return early(sz, bounds[i], bounds[i - 1] if i else None, pattern, green,
                     upto(dist, last_e), slots[:s + 1], total)

    total = part(0, None)
    extra = []
    if sz.half > fixed:
        full = jnp.bool_(False)
        for c in range(sz.cols):
            other = (1 - c) * sz.half
            full = jnp.logical_or(full, jnp.all(pattern[c, other:other + sz.half] > 0))

        def more(g):
            return lax.ppermute(pick(sz, fixed, pattern, g), "col", swap)

        full, total = lax.optimization_barrier((full, total))
        got = lax.cond(full, more, lambda g: jnp.zeros((sz.local_rows, block), BF16), green)
        got, total = lax.optimization_barrier((got, total))
        extra.append(got)
    total = part(1, total)
    near = (far, per_row - 2, sz.half)
    *out, total = late_diag(sz, near, bounds[1], pattern, pole_weight, green, upto(far, per_row - 2),
                            slots + extra, total, factor, diag_inverse, far_term)
    last = (far, per_row - 1, sz.half)
    only = {k: v for k, v in m.items() if abs(k // per_row) == far and k % per_row == per_row - 1}
    off_out = late_off(sz, last, near, pattern, pole_weight, green, only, slots + extra, total)

    def swapped(axis, sends, perms):
        ins = []
        for v, perm in zip(sends, perms):
            ins.append(lax.ppermute(v, axis, perm))
        return ins

    diag, *sends = out
    diag_in = swapped("pole", sends, [pole_perm(sz, step) for step in pole_steps(sz)])
    off, *sends = off_out
    off_in = swapped("pole", sends, shifts(sz.poles, sz.cores, 1))
    off, *sends = fold(sz.outer, "pole", sz.cores, off, off_in)
    off_in = swapped("pole", sends, shifts(sz.poles, sz.outer, sz.cores))
    diag, *sends = fold(sz.rows, "row", 1, diag, diag_in)
    diag_in = swapped("row", sends, shifts(sz.rows, sz.rows, 1))
    for v in off_in:
        off = off + v.astype(F32)
    for v in diag_in:
        diag = diag + v.astype(F32)
    return off, diag


def make_body(mesh):
    def body(green, factor, diag_inverse, pole_weight, pattern):
        sz = Sizes(mesh, green, factor, diag_inverse, pattern)
        fits = sz.cols == 2 and sz.level == 1 and sz.cores == 2 and sz.rows >= 4 and sz.block % (sz.local_rows // sz.poles) == 0 and sz.per_row >= 2 and sz.half >= 3
        if not fits:
            return generic(sz, green, factor, diag_inverse, pole_weight, pattern)
        return blocked(sz, green, factor, diag_inverse, pole_weight, pattern)

    return body


def solution(mesh):
    in_specs = (
        P("pole", "row", "col"),
        P("pole", "row", "col"),
        P("pole", "row", "col"),
        P("pole"),
        P(),
    )
    out_specs = (P(("row", "pole"), "col"), P(("pole", "row"), "col"))
    return jax.shard_map(make_body(mesh), mesh=mesh, in_specs=in_specs, out_specs=out_specs, check_vma=False)
```

```python
import functools

import jax
import jax.numpy as jnp
from jax import lax
from jax.experimental import pallas as pl
from jax.experimental.pallas import tpu as pltpu
from jax.sharding import PartitionSpec as P


VMEM = pl.BlockSpec(memory_space=pltpu.VMEM)
SMEM = pl.BlockSpec(memory_space=pltpu.SMEM)
ANY = pl.BlockSpec(memory_space=pltpu.HBM)
SMALL = pltpu.CompilerParams(vmem_limit_bytes=12 * 2**20)
F32 = jnp.float32
BF16 = jnp.bfloat16


class Sizes:
    def __init__(self, mesh, green, factor, diag_inverse, pattern):
        self.poles, self.rows, self.cols = (mesh.shape[a] for a in ("pole", "row", "col"))
        self.local_rows, self.k_local = green.shape[1], green.shape[2]
        self.width = factor.shape[2]
        self.anc, supers = pattern.shape
        self.block = self.local_rows * self.rows // self.anc
        self.per_row = self.local_rows // self.block
        self.half = self.k_local // self.block
        self.level = supers // self.cols
        self.count = diag_inverse.shape[1]
        self.cores = 2 if self.poles % 2 == 0 else 1
        self.outer = self.poles // self.cores


def swap_sum(part, axis, size, group, stride, held_as):
    at = lax.axis_index(axis)
    digit = (at // stride) % group
    total = lax.dynamic_index_in_dim(part, digit, 0, keepdims=False)
    for step in range(1, group):
        perm = []
        for i in range(size):
            d = (i // stride) % group
            perm.append((i, i + ((d + step) % group - d) * stride))
        to = (digit + step) % group
        send = lax.dynamic_index_in_dim(part, to, 0, keepdims=False).astype(held_as)
        total = total + lax.ppermute(send, axis, perm).astype(F32)
    return total


def generic(sz, green, factor, diag_inverse, pole_weight, pattern):
    block, per_row, cols = sz.block, sz.per_row, sz.width
    row_at = lax.axis_index("row")
    col_at = lax.axis_index("col")
    pattern_f = pattern.astype(F32)
    here = lax.dynamic_slice(pattern_f, (0, col_at * sz.level), (sz.anc, sz.level))
    keep = jnp.repeat(here, block, axis=1)
    own_keep = lax.dynamic_slice_in_dim(keep, row_at * per_row, per_row, 0)
    weight = pole_weight[0]
    gl = green[0]
    fac = factor[0].reshape(per_row, block, cols)
    got = {}
    for shift in range(1, sz.cols):
        perm = [(i, (i + shift) % sz.cols) for i in range(sz.cols)]
        for j in range(sz.half):
            got[shift, j] = lax.ppermute(gl[:, j * block:(j + 1) * block], "col", perm)
    right = [(i, i + 1) for i in range(sz.rows - 1)]
    left = [(i + 1, i) for i in range(sz.rows - 1)]
    blocks = {(0, e): fac[e] for e in range(per_row)}
    from_left, from_right = {}, {}
    for e in range(per_row):
        a = b = fac[e]
        for step in range(1, sz.rows):
            from_left[step, e] = a = lax.ppermute(a, "row", right)
            from_right[step, e] = b = lax.ppermute(b, "row", left)
    for step in range(1, sz.rows):
        for e in range(per_row):
            blocks[step, e] = jnp.where(row_at >= step, from_left[step, e], from_right[sz.rows - step, e])
    stacked = jnp.stack([blocks[s, e] for s in range(sz.rows) for e in range(per_row)])

    def factor_of(a):
        at = ((row_at - a // per_row) % sz.rows) * per_row + a % per_row
        kept = lax.dynamic_index_in_dim(keep, a, 0).astype(BF16)
        return lax.dynamic_index_in_dim(stacked, at, 0, keepdims=False) * kept

    product = jnp.zeros((sz.local_rows, cols), F32)
    for shift in range(sz.cols):
        for j in range(sz.half):
            src = (col_at - shift) % sz.cols
            g = gl[:, j * block:(j + 1) * block] if shift == 0 else got[shift, j]
            product += jnp.dot(g, factor_of(src * sz.half + j), preferred_element_type=F32)
    product = product.reshape(per_row, block, cols) * own_keep[:, None, :]
    update = product.astype(BF16).reshape(sz.local_rows, sz.level, block)
    masked = (fac * own_keep.astype(BF16)[:, None, :]).reshape(sz.local_rows, sz.level, block)
    cross = jnp.einsum("rka,rkb->akb", masked, update, preferred_element_type=F32).reshape(block, cols)
    diag = -weight * cross
    mine = lax.dynamic_slice_in_dim(diag, row_at * sz.count, sz.count, 0)
    mine = mine + weight * diag_inverse[0].astype(F32)
    diag = lax.dynamic_update_slice_in_dim(diag, mine, row_at * sz.count, 0)
    off = -weight * product.reshape(sz.local_rows, cols)
    res = []
    for x in (diag, off):
        r = x.shape[0] // sz.poles
        x = x.reshape(sz.outer, sz.cores, r, cols).transpose(1, 0, 2, 3)
        x = swap_sum(x, "pole", sz.poles, sz.cores, 1, BF16)
        res.append(swap_sum(x, "pole", sz.poles, sz.outer, sz.cores, BF16))
    diag, off = res
    return off, swap_sum(diag.reshape(sz.rows, -1, cols), "row", sz.rows, sz.rows, 1, BF16)


def swap_ranks(sz, pat, row, to):
    base = (1 - to) * sz.half
    need, dist = [], []
    for j in range(sz.half):
        need.append(pat[to, base + j])
        dist.append(jnp.abs((base + j) // sz.per_row - row))
    rank = []
    for j in range(sz.half):
        n = jnp.int32(0)
        for i in range(sz.half):
            if i != j:
                before = dist[i] > dist[j] if i < j else dist[i] >= dist[j]
                n = n + jnp.where(before, need[i], 0)
        rank.append(n)
    return need, rank


def pick_kernel(sz, slot, parts, pat, green, out, buf, in_sem, out_sem):
    need, rank = swap_ranks(sz, pat, lax.axis_index("row"), 1 - lax.axis_index("col"))
    at = jnp.int32(0)
    for j in range(sz.half):
        at = jnp.where(jnp.logical_and(need[j] > 0, rank[j] == slot), j, at)
    at = pl.multiple_of(at * sz.block, sz.block)
    n = sz.local_rows // parts
    ins, outs = [], []
    for i in range(parts):
        ins.append(pltpu.make_async_copy(green.at[0, pl.ds(i * n, n), pl.ds(at, sz.block)], buf.at[i], in_sem.at[i]))
        outs.append(pltpu.make_async_copy(buf.at[i], out.at[pl.ds(i * n, n)], out_sem.at[i]))
        ins[i].start()
    for i in range(parts):
        ins[i].wait()
        outs[i].start()
    for i in range(parts):
        outs[i].wait()


def pick(sz, slot, pattern, green):
    parts = 4
    return pl.pallas_call(
        functools.partial(pick_kernel, sz, slot, parts),
        out_shape=jax.ShapeDtypeStruct((sz.local_rows, sz.block), BF16),
        in_specs=[SMEM, ANY],
        out_specs=ANY,
        scratch_shapes=[
            pltpu.VMEM((parts, sz.local_rows // parts, sz.block), BF16),
            pltpu.SemaphoreType.DMA((parts,)),
            pltpu.SemaphoreType.DMA((parts,)),
        ],
        compiler_params=SMALL,
    )(pattern, *in_hbm([green]))


def product_jobs(sz, pat, ready, before, m_refs, g_local, g_slots, job, bufs, total):
    m_buf, g_buf, m_sem, g_sem = bufs
    row, col = lax.axis_index("row"), lax.axis_index("col")
    _, rank = swap_ranks(sz, pat, row, col)

    def inside(bound, dist, e, slot):
        if bound is None:
            return jnp.bool_(False)
        d, last_e, s = bound
        near = jnp.logical_or(dist < d, jnp.logical_and(dist == d, e <= last_e))
        return jnp.logical_and(near, slot <= s)

    count = jnp.int32(0)
    for a in range(sz.anc):
        away = a // sz.per_row - row
        dist, e = jnp.abs(away), a % sz.per_row
        local = (a // sz.half) == col
        slot = jnp.where(local, -1, rank[a % sz.half])
        todo = jnp.logical_and(inside(ready, dist, e, slot), jnp.logical_not(inside(before, dist, e, slot)))
        todo = jnp.logical_and(todo, pat[col, a] > 0)

        @pl.when(todo)
        def _(a=a, count=count, slot=slot, away=away):
            job[0, count] = away * sz.per_row + a % sz.per_row
            job[1, count] = slot
            job[2, count] = a % sz.half

        count = count + jnp.where(todo, 1, 0)

    def fetch(n, into):
        for key, ref in m_refs.items():
            @pl.when(job[0, n] == key)
            def _(ref=ref):
                pltpu.make_async_copy(ref, m_buf.at[into], m_sem.at[into]).start()

        @pl.when(job[1, n] < 0)
        def _():
            at = pl.multiple_of(job[2, n] * sz.block, sz.block)
            pltpu.make_async_copy(g_local.at[0, :, pl.ds(at, sz.block)], g_buf.at[into], g_sem.at[into]).start()

        for s, ref in enumerate(g_slots):
            @pl.when(job[1, n] == s)
            def _(ref=ref):
                pltpu.make_async_copy(ref, g_buf.at[into], g_sem.at[into]).start()

    @pl.when(count > 0)
    def _():
        fetch(0, 0)

    def step(n, carry):
        now = lax.rem(n, 2)

        @pl.when(n + 1 < count)
        def _():
            fetch(n + 1, 1 - now)

        pltpu.make_async_copy(m_buf.at[now], m_buf.at[now], m_sem.at[now]).wait()
        pltpu.make_async_copy(g_buf.at[now], g_buf.at[now], g_sem.at[now]).wait()
        total[...] += jnp.dot(g_buf[now], m_buf[now], preferred_element_type=F32)
        return carry

    lax.fori_loop(0, count, step, 0)


def in_hbm(arrays):
    return [pltpu.with_memory_space_constraint(a, pltpu.HBM) for a in arrays]


def job_scratch(sz):
    return [
        pltpu.SMEM((3, sz.anc), jnp.int32),
        pltpu.VMEM((2, sz.block, sz.width), BF16),
        pltpu.VMEM((2, sz.local_rows, sz.block), BF16),
        pltpu.SemaphoreType.DMA((2,)),
        pltpu.SemaphoreType.DMA((2,)),
    ]


def early_kernel(sz, ready, before, keys, n_slots, first, pat, g_local, *refs):
    refs = list(refs)
    m_refs = {k: refs.pop(0) for k in keys}
    g_slots = [refs.pop(0) for _ in range(n_slots)]
    total_in = None if first else refs.pop(0)
    out = refs.pop(0)
    job, m_buf, g_buf, m_sem, g_sem = refs
    if first:
        out[...] = jnp.zeros_like(out)
    else:
        out[...] = total_in[...]
    product_jobs(sz, pat, ready, before, m_refs, g_local, g_slots, job, (m_buf, g_buf, m_sem, g_sem), out)


def early(sz, ready, before, pattern, green, m, slots, total):
    keys = list(m)
    first = total is None
    args = [pattern] + in_hbm([green] + [m[k] for k in keys] + list(slots)) + ([] if first else [total])
    return early_call(sz, ready, before, keys, slots, first, args)


def early_call(sz, ready, before, keys, slots, first, args):
    return pl.pallas_call(
        functools.partial(early_kernel, sz, ready, before, keys, len(slots), first),
        out_shape=jax.ShapeDtypeStruct((sz.local_rows, sz.width), F32),
        in_specs=[SMEM] + [ANY] * (1 + len(keys) + len(slots)) + ([] if first else [VMEM]),
        out_specs=VMEM,
        scratch_shapes=job_scratch(sz),
        input_output_aliases={} if first else {len(args) - 1: 0},
        compiler_params=SMALL,
    )(*args)


def far_block(sz, row):
    far = jnp.where(row < sz.rows // 2, sz.rows - 1, 0)
    return far * sz.per_row + sz.per_row - 1


def inner_kernel(sz, pat, green, slot, factor, out, g_buf, sem):
    row, col = lax.axis_index("row"), lax.axis_index("col")
    a = far_block(sz, row)

    @pl.when(a // sz.half == col)
    def _():
        at = pl.multiple_of(lax.rem(a, sz.half) * sz.block, sz.block)
        pltpu.make_async_copy(green.at[0, :, pl.ds(at, sz.block)], g_buf, sem).start()

    @pl.when(a // sz.half != col)
    def _():
        pltpu.make_async_copy(slot, g_buf, sem).start()

    pltpu.make_async_copy(g_buf, g_buf, sem).wait()
    total = jnp.zeros((sz.width, sz.block), F32)
    for e in range(sz.per_row):
        at = pl.ds(e * sz.block, sz.block)
        kept = pat[col, row * sz.per_row + e] > 0
        part = lax.dot_general(factor[0, at, :], g_buf[at, :], (((0,), (0,)), ((), ())), preferred_element_type=F32)
        total = total + jnp.where(kept, part, 0.0)
    out[...] = total.astype(BF16)


def inner(sz, pattern, green, slot, factor):
    return pl.pallas_call(
        functools.partial(inner_kernel, sz),
        out_shape=jax.ShapeDtypeStruct((sz.width, sz.block), BF16),
        in_specs=[SMEM, ANY, ANY, VMEM],
        out_specs=VMEM,
        scratch_shapes=[pltpu.VMEM((sz.local_rows, sz.block), BF16), pltpu.SemaphoreType.DMA],
        compiler_params=SMALL,
        name="inner",
    )(pattern, *in_hbm([green, slot]), factor)


def late_diag_kernel(sz, ready, before, keys, n_slots, pat, weight, g_local, *refs):
    refs = list(refs)
    m_refs = {k: refs.pop(0) for k in keys}
    g_slots = [refs.pop(0) for _ in range(n_slots)]
    total_in, factor, dinv, far_term = (refs.pop(0) for _ in range(4))
    outs = [refs.pop(0) for _ in range(sz.cores)]
    total, diag = refs.pop(0), refs.pop(0)
    job, m_buf, g_buf, m_sem, g_sem = refs
    row, col = lax.axis_index("row"), lax.axis_index("col")
    core = lax.rem(lax.axis_index("pole"), sz.cores)

    away = sz.rows - 2
    for at_row, sign in ((1, 1), (sz.rows - 2, -1)):
        key = sign * away * sz.per_row + sz.per_row - 1

        @pl.when(row == at_row)
        def _(key=key):
            copy = pltpu.make_async_copy(m_refs[key], m_buf.at[0], m_sem.at[0])
            copy.start()
            copy.wait()

    inward = jnp.logical_or(row == 1, row == sz.rows - 2)
    a = far_block(sz, row)
    w = weight[0]
    diag[...] = jnp.zeros_like(diag)

    @pl.when(jnp.logical_and(inward, pat[col, a] > 0))
    def _():
        diag[...] -= w * jnp.dot(far_term[...], m_buf[0], preferred_element_type=F32)

    total[...] = total_in[...]
    product_jobs(sz, pat, ready, before, m_refs, g_local, g_slots, job, (m_buf, g_buf, m_sem, g_sem), total)
    for e in range(sz.per_row):
        at = pl.ds(e * sz.block, sz.block)

        @pl.when(pat[col, row * sz.per_row + e] > 0)
        def _(at=at):
            diag[...] -= w * lax.dot_general(
                factor[0, at, :], total[at, :].astype(BF16), (((0,), (0,)), ((), ())), preferred_element_type=F32)

    mine = pl.ds(pl.multiple_of(row * sz.count, sz.count), sz.count)
    diag[mine, :] += w * dinv[0].astype(F32)
    n = diag.shape[0] // sz.poles
    for dc, out in enumerate(outs):
        for x in range(sz.outer):
            q = x * sz.cores + lax.rem(core + dc, sz.cores)
            out[x * n:(x + 1) * n, :] = diag[pl.ds(pl.multiple_of(q * n, n), n), :].astype(out.dtype)


def late_diag(sz, ready, before, pattern, weight, green, m, slots, landed, total, factor, dinv, far_term):
    keys = list(m)
    args = [pattern, weight] + in_hbm([green] + [m[k] for k in keys])
    args += [v if s == landed else in_hbm([v])[0] for s, v in enumerate(slots)] + [total, factor, dinv, far_term]
    shapes = [jax.ShapeDtypeStruct((sz.block // sz.cores, sz.width), BF16 if i else F32) for i in range(sz.cores)]
    shapes.append(jax.ShapeDtypeStruct((sz.local_rows, sz.width), F32))
    return pl.pallas_call(
        functools.partial(late_diag_kernel, sz, ready, before, keys, len(slots)),
        out_shape=shapes,
        in_specs=[SMEM] * 2 + [ANY] * (1 + len(keys))
        + [VMEM if s == landed else ANY for s in range(len(slots))] + [VMEM] * 4,
        out_specs=[VMEM] * (sz.cores + 1),
        scratch_shapes=[pltpu.VMEM((sz.block, sz.width), F32)] + job_scratch(sz),
        compiler_params=SMALL,
        name="late_diag",
    )(*args)


def late_off_kernel(sz, ready, before, keys, n_slots, pat, weight, g_local, *refs):
    refs = list(refs)
    m_refs = {k: refs.pop(0) for k in keys}
    g_slots = [refs.pop(0) for _ in range(n_slots)]
    total_in = refs.pop(0)
    outs = [refs.pop(0) for _ in range(sz.cores)]
    total = refs.pop(0)
    job, m_buf, g_buf, m_sem, g_sem = refs
    row, col = lax.axis_index("row"), lax.axis_index("col")
    core = lax.rem(lax.axis_index("pole"), sz.cores)
    total[...] = total_in[...]
    product_jobs(sz, pat, ready, before, m_refs, g_local, g_slots, job, (m_buf, g_buf, m_sem, g_sem), total)
    w = weight[0]
    n = total.shape[0] // sz.poles
    for dc, out in enumerate(outs):
        for x in range(sz.outer):
            q = x * sz.cores + lax.rem(core + dc, sz.cores)
            kept = pat[col, row * sz.per_row + (q * n) // sz.block] > 0
            v = total[pl.ds(pl.multiple_of(q * n, n), n), :]
            out[x * n:(x + 1) * n, :] = jnp.where(kept, -w * v, 0.0).astype(out.dtype)


def late_off(sz, ready, before, pattern, weight, green, m, slots, total):
    keys = list(m)
    args = [pattern, weight] + in_hbm([green] + [m[k] for k in keys] + list(slots)) + [total]
    shapes = [jax.ShapeDtypeStruct((sz.local_rows // sz.cores, sz.width), BF16 if i else F32) for i in range(sz.cores)]
    return pl.pallas_call(
        functools.partial(late_off_kernel, sz, ready, before, keys, len(slots)),
        out_shape=shapes,
        in_specs=[SMEM] * 2 + [ANY] * (1 + len(keys) + len(slots)) + [VMEM],
        out_specs=[VMEM] * sz.cores,
        scratch_shapes=[pltpu.VMEM((sz.local_rows, sz.width), F32)] + job_scratch(sz),
        compiler_params=SMALL,
        name="late_off",
    )(*args)


def fold_kernel(group, n_in, axis, stride, keep, *refs):
    ins, outs = refs[:n_in], refs[n_in:]
    own, sends = outs[0], outs[1:]
    n = own.shape[0]
    me = lax.rem(lax.axis_index(axis) // stride, group)

    def part(d):
        at = pl.ds(pl.multiple_of(d * n, n), n)
        v = keep[at, :]
        for r in ins:
            v = v + r[at, :].astype(F32)
        return v

    for s, send in enumerate(sends):
        send[...] = part(lax.rem(me + s + 1, group)).astype(BF16)
    own[...] = part(me)


def fold(group, axis, stride, keep, ins):
    n, width = keep.shape[0] // group, keep.shape[1]
    shapes = [jax.ShapeDtypeStruct((n, width), F32)] + [jax.ShapeDtypeStruct((n, width), BF16)] * (group - 1)
    return pl.pallas_call(
        functools.partial(fold_kernel, group, len(ins), axis, stride),
        out_shape=shapes,
        in_specs=[VMEM] * (1 + len(ins)),
        out_specs=[VMEM] * group,
        compiler_params=SMALL,
    )(keep, *ins)


def shifts(size, group, stride):
    perms = []
    for step in range(1, group):
        perm = []
        for i in range(size):
            d = (i // stride) % group
            perm.append((i, i + ((d + step) % group - d) * stride))
        perms.append(perm)
    return perms


def blocked(sz, green, factor, diag_inverse, pole_weight, pattern):
    block, per_row = sz.block, sz.per_row
    pattern = pattern.T
    fac = [factor[0, e * block:(e + 1) * block] for e in range(per_row)]
    swap = [(0, 1), (1, 0)]

    fixed = max(sz.half - 1, 1)
    slots = []
    for s in range(fixed):
        sent = pick(sz, s, pattern, green)
        slots.append(lax.ppermute(sent, "col", swap))

    m = {e: fac[e] for e in range(per_row)}
    for e in range(per_row):
        a = b = fac[e]
        for step in range(1, sz.rows):
            m[-step * per_row + e] = a = lax.ppermute(a, "row", [(i, i + 1) for i in range(step - 1, sz.rows - 1)])
            m[step * per_row + e] = b = lax.ppermute(b, "row", [(i + 1, i) for i in range(sz.rows - step)])

    def upto(dist, last_e):
        return {k: v for k, v in m.items() if abs(k // per_row) < dist or (abs(k // per_row) == dist and k % per_row <= last_e)}

    far = sz.rows - 1
    bounds = [(far - 2, per_row - 1, 0), (far - 1, per_row - 1, fixed - 2), (far, per_row - 2, fixed - 2)]
    far_term = inner(sz, pattern, green, slots[0], factor)
    far_term = lax.ppermute(far_term, "row", [(0, 1), (far, far - 1)])

    def part(i, total):
        dist, last_e, s = bounds[i]
        return early(sz, bounds[i], bounds[i - 1] if i else None, pattern, green,
                     upto(dist, last_e), slots[:s + 1], total)

    total = part(1, part(0, None))
    extra = []
    if sz.half > fixed:
        full = jnp.bool_(False)
        for c in range(sz.cols):
            other = (1 - c) * sz.half
            full = jnp.logical_or(full, jnp.all(pattern[c, other:other + sz.half] > 0))

        def more(g):
            return lax.ppermute(pick(sz, fixed, pattern, g), "col", swap)

        full, total = lax.optimization_barrier((full, total))
        got = lax.cond(full, more, lambda g: jnp.zeros((sz.local_rows, block), BF16), green)
        got, total = lax.optimization_barrier((got, total))
        extra.append(got)
    total = part(2, total)
    near = (far, per_row - 2, sz.half)
    *out, total = late_diag(sz, near, bounds[2], pattern, pole_weight, green, upto(far, per_row - 2),
                            slots + extra, fixed - 1, total, factor, diag_inverse, far_term)
    last = (far, per_row - 1, sz.half)
    only = {k: v for k, v in m.items() if abs(k // per_row) == far and k % per_row == per_row - 1}
    off_out = late_off(sz, last, near, pattern, pole_weight, green, only, slots + extra, total)

    def swapped(axis, sends, perms):
        ins = []
        for v, perm in zip(sends, perms):
            ins.append(lax.ppermute(v, axis, perm))
        return ins

    diag, *sends = out
    diag_in = swapped("pole", sends, shifts(sz.poles, sz.cores, 1))
    diag, *sends = fold(sz.outer, "pole", sz.cores, diag, diag_in)
    diag_in = swapped("pole", sends, shifts(sz.poles, sz.outer, sz.cores))
    off, *sends = off_out
    off_in = swapped("pole", sends, shifts(sz.poles, sz.cores, 1))
    off, *sends = fold(sz.outer, "pole", sz.cores, off, off_in)
    off_in = swapped("pole", sends, shifts(sz.poles, sz.outer, sz.cores))
    diag, *sends = fold(sz.rows, "row", 1, diag, diag_in)
    diag_in = swapped("row", sends, shifts(sz.rows, sz.rows, 1))
    for v in off_in:
        off = off + v.astype(F32)
    for v in diag_in:
        diag = diag + v.astype(F32)
    return off, diag


def make_body(mesh):
    def body(green, factor, diag_inverse, pole_weight, pattern):
        sz = Sizes(mesh, green, factor, diag_inverse, pattern)
        fits = sz.cols == 2 and sz.level == 1 and sz.cores == 2 and sz.rows >= 4 and sz.block % (sz.local_rows // sz.poles) == 0 and sz.per_row >= 2 and sz.half >= 3
        if not fits:
            return generic(sz, green, factor, diag_inverse, pole_weight, pattern)
        return blocked(sz, green, factor, diag_inverse, pole_weight, pattern)

    return body


def solution(mesh):
    in_specs = (
        P("pole", "row", "col"),
        P("pole", "row", "col"),
        P("pole", "row", "col"),
        P("pole"),
        P(),
    )
    out_specs = (P(("row", "pole"), "col"), P(("pole", "row"), "col"))
    return jax.shard_map(make_body(mesh), mesh=mesh, in_specs=in_specs, out_specs=out_specs, check_vma=False)
```

```python
import functools

import jax
import jax.numpy as jnp
from jax import lax
from jax.experimental import pallas as pl
from jax.experimental.pallas import tpu as pltpu
from jax.sharding import PartitionSpec as P


VMEM = pl.BlockSpec(memory_space=pltpu.VMEM)
SMEM = pl.BlockSpec(memory_space=pltpu.SMEM)
ANY = pl.BlockSpec(memory_space=pltpu.HBM)
SMALL = pltpu.CompilerParams(vmem_limit_bytes=12 * 2**20)
F32 = jnp.float32
BF16 = jnp.bfloat16


class Sizes:
    def __init__(self, mesh, green, factor, diag_inverse, pattern):
        self.poles, self.rows, self.cols = (mesh.shape[a] for a in ("pole", "row", "col"))
        self.local_rows, self.k_local = green.shape[1], green.shape[2]
        self.width = factor.shape[2]
        self.anc, supers = pattern.shape
        self.block = self.local_rows * self.rows // self.anc
        self.per_row = self.local_rows // self.block
        self.half = self.k_local // self.block
        self.level = supers // self.cols
        self.count = diag_inverse.shape[1]
        self.cores = 2 if self.poles % 2 == 0 else 1
        self.outer = self.poles // self.cores


def swap_sum(part, axis, size, group, stride, held_as):
    at = lax.axis_index(axis)
    digit = (at // stride) % group
    total = lax.dynamic_index_in_dim(part, digit, 0, keepdims=False)
    for step in range(1, group):
        perm = []
        for i in range(size):
            d = (i // stride) % group
            perm.append((i, i + ((d + step) % group - d) * stride))
        to = (digit + step) % group
        send = lax.dynamic_index_in_dim(part, to, 0, keepdims=False).astype(held_as)
        total = total + lax.ppermute(send, axis, perm).astype(F32)
    return total


def generic(sz, green, factor, diag_inverse, pole_weight, pattern):
    block, per_row, cols = sz.block, sz.per_row, sz.width
    row_at = lax.axis_index("row")
    col_at = lax.axis_index("col")
    pattern_f = pattern.astype(F32)
    here = lax.dynamic_slice(pattern_f, (0, col_at * sz.level), (sz.anc, sz.level))
    keep = jnp.repeat(here, block, axis=1)
    own_keep = lax.dynamic_slice_in_dim(keep, row_at * per_row, per_row, 0)
    weight = pole_weight[0]
    gl = green[0]
    fac = factor[0].reshape(per_row, block, cols)
    got = {}
    for shift in range(1, sz.cols):
        perm = [(i, (i + shift) % sz.cols) for i in range(sz.cols)]
        for j in range(sz.half):
            got[shift, j] = lax.ppermute(gl[:, j * block:(j + 1) * block], "col", perm)
    right = [(i, i + 1) for i in range(sz.rows - 1)]
    left = [(i + 1, i) for i in range(sz.rows - 1)]
    blocks = {(0, e): fac[e] for e in range(per_row)}
    from_left, from_right = {}, {}
    for e in range(per_row):
        a = b = fac[e]
        for step in range(1, sz.rows):
            from_left[step, e] = a = lax.ppermute(a, "row", right)
            from_right[step, e] = b = lax.ppermute(b, "row", left)
    for step in range(1, sz.rows):
        for e in range(per_row):
            blocks[step, e] = jnp.where(row_at >= step, from_left[step, e], from_right[sz.rows - step, e])
    stacked = jnp.stack([blocks[s, e] for s in range(sz.rows) for e in range(per_row)])

    def factor_of(a):
        at = ((row_at - a // per_row) % sz.rows) * per_row + a % per_row
        kept = lax.dynamic_index_in_dim(keep, a, 0).astype(BF16)
        return lax.dynamic_index_in_dim(stacked, at, 0, keepdims=False) * kept

    product = jnp.zeros((sz.local_rows, cols), F32)
    for shift in range(sz.cols):
        for j in range(sz.half):
            src = (col_at - shift) % sz.cols
            g = gl[:, j * block:(j + 1) * block] if shift == 0 else got[shift, j]
            product += jnp.dot(g, factor_of(src * sz.half + j), preferred_element_type=F32)
    product = product.reshape(per_row, block, cols) * own_keep[:, None, :]
    update = product.astype(BF16).reshape(sz.local_rows, sz.level, block)
    masked = (fac * own_keep.astype(BF16)[:, None, :]).reshape(sz.local_rows, sz.level, block)
    cross = jnp.einsum("rka,rkb->akb", masked, update, preferred_element_type=F32).reshape(block, cols)
    diag = -weight * cross
    mine = lax.dynamic_slice_in_dim(diag, row_at * sz.count, sz.count, 0)
    mine = mine + weight * diag_inverse[0].astype(F32)
    diag = lax.dynamic_update_slice_in_dim(diag, mine, row_at * sz.count, 0)
    off = -weight * product.reshape(sz.local_rows, cols)
    res = []
    for x in (diag, off):
        r = x.shape[0] // sz.poles
        x = x.reshape(sz.outer, sz.cores, r, cols).transpose(1, 0, 2, 3)
        x = swap_sum(x, "pole", sz.poles, sz.cores, 1, BF16)
        res.append(swap_sum(x, "pole", sz.poles, sz.outer, sz.cores, BF16))
    diag, off = res
    return off, swap_sum(diag.reshape(sz.rows, -1, cols), "row", sz.rows, sz.rows, 1, BF16)


def swap_ranks(sz, pat, row, to):
    base = (1 - to) * sz.half
    need, dist = [], []
    for j in range(sz.half):
        need.append(pat[to, base + j])
        dist.append(jnp.abs((base + j) // sz.per_row - row))
    rank = []
    for j in range(sz.half):
        n = jnp.int32(0)
        for i in range(sz.half):
            if i != j:
                before = dist[i] > dist[j] if i < j else dist[i] >= dist[j]
                n = n + jnp.where(before, need[i], 0)
        rank.append(n)
    return need, rank


def pick_kernel(sz, slot, parts, pat, green, out, buf, in_sem, out_sem):
    need, rank = swap_ranks(sz, pat, lax.axis_index("row"), 1 - lax.axis_index("col"))
    at = jnp.int32(0)
    for j in range(sz.half):
        at = jnp.where(jnp.logical_and(need[j] > 0, rank[j] == slot), j, at)
    at = pl.multiple_of(at * sz.block, sz.block)
    n = sz.local_rows // parts
    ins, outs = [], []
    for i in range(parts):
        ins.append(pltpu.make_async_copy(green.at[0, pl.ds(i * n, n), pl.ds(at, sz.block)], buf.at[i], in_sem.at[i]))
        outs.append(pltpu.make_async_copy(buf.at[i], out.at[pl.ds(i * n, n)], out_sem.at[i]))
        ins[i].start()
    for i in range(parts):
        ins[i].wait()
        outs[i].start()
    for i in range(parts):
        outs[i].wait()


def pick(sz, slot, pattern, green):
    parts = 4
    return pl.pallas_call(
        functools.partial(pick_kernel, sz, slot, parts),
        out_shape=jax.ShapeDtypeStruct((sz.local_rows, sz.block), BF16),
        in_specs=[SMEM, ANY],
        out_specs=ANY,
        scratch_shapes=[
            pltpu.VMEM((parts, sz.local_rows // parts, sz.block), BF16),
            pltpu.SemaphoreType.DMA((parts,)),
            pltpu.SemaphoreType.DMA((parts,)),
        ],
        compiler_params=SMALL,
    )(pattern, *in_hbm([green]))


def product_jobs(sz, pat, ready, before, m_refs, g_local, g_slots, job, bufs, total):
    m_buf, g_buf, m_sem, g_sem = bufs
    row, col = lax.axis_index("row"), lax.axis_index("col")
    _, rank = swap_ranks(sz, pat, row, col)

    def inside(bound, dist, e, slot):
        if bound is None:
            return jnp.bool_(False)
        d, last_e, s = bound
        near = jnp.logical_or(dist < d, jnp.logical_and(dist == d, e <= last_e))
        return jnp.logical_and(near, slot <= s)

    count = jnp.int32(0)
    for a in range(sz.anc):
        away = a // sz.per_row - row
        dist, e = jnp.abs(away), a % sz.per_row
        local = (a // sz.half) == col
        slot = jnp.where(local, -1, rank[a % sz.half])
        todo = jnp.logical_and(inside(ready, dist, e, slot), jnp.logical_not(inside(before, dist, e, slot)))
        todo = jnp.logical_and(todo, pat[col, a] > 0)

        @pl.when(todo)
        def _(a=a, count=count, slot=slot, away=away):
            job[0, count] = away * sz.per_row + a % sz.per_row
            job[1, count] = slot
            job[2, count] = a % sz.half

        count = count + jnp.where(todo, 1, 0)

    def fetch(n, into):
        for key, ref in m_refs.items():
            @pl.when(job[0, n] == key)
            def _(ref=ref):
                pltpu.make_async_copy(ref, m_buf.at[into], m_sem.at[into]).start()

        @pl.when(job[1, n] < 0)
        def _():
            at = pl.multiple_of(job[2, n] * sz.block, sz.block)
            pltpu.make_async_copy(g_local.at[0, :, pl.ds(at, sz.block)], g_buf.at[into], g_sem.at[into]).start()

        for s, ref in enumerate(g_slots):
            @pl.when(job[1, n] == s)
            def _(ref=ref):
                pltpu.make_async_copy(ref, g_buf.at[into], g_sem.at[into]).start()

    @pl.when(count > 0)
    def _():
        fetch(0, 0)

    def step(n, carry):
        now = lax.rem(n, 2)

        @pl.when(n + 1 < count)
        def _():
            fetch(n + 1, 1 - now)

        pltpu.make_async_copy(m_buf.at[now], m_buf.at[now], m_sem.at[now]).wait()
        pltpu.make_async_copy(g_buf.at[now], g_buf.at[now], g_sem.at[now]).wait()
        total[...] += jnp.dot(g_buf[now], m_buf[now], preferred_element_type=F32)
        return carry

    lax.fori_loop(0, count, step, 0)


def in_hbm(arrays):
    return [pltpu.with_memory_space_constraint(a, pltpu.HBM) for a in arrays]


def job_scratch(sz):
    return [
        pltpu.SMEM((3, sz.anc), jnp.int32),
        pltpu.VMEM((2, sz.block, sz.width), BF16),
        pltpu.VMEM((2, sz.local_rows, sz.block), BF16),
        pltpu.SemaphoreType.DMA((2,)),
        pltpu.SemaphoreType.DMA((2,)),
    ]


def early_kernel(sz, ready, before, keys, n_slots, first, pat, g_local, *refs):
    refs = list(refs)
    m_refs = {k: refs.pop(0) for k in keys}
    g_slots = [refs.pop(0) for _ in range(n_slots)]
    total_in = None if first else refs.pop(0)
    out = refs.pop(0)
    job, m_buf, g_buf, m_sem, g_sem = refs
    if first:
        out[...] = jnp.zeros_like(out)
    else:
        out[...] = total_in[...]
    product_jobs(sz, pat, ready, before, m_refs, g_local, g_slots, job, (m_buf, g_buf, m_sem, g_sem), out)


def early(sz, ready, before, pattern, green, m, slots, total):
    keys = list(m)
    first = total is None
    args = [pattern] + in_hbm([green] + [m[k] for k in keys] + list(slots)) + ([] if first else [total])
    return early_call(sz, ready, before, keys, slots, first, args)


def early_call(sz, ready, before, keys, slots, first, args):
    return pl.pallas_call(
        functools.partial(early_kernel, sz, ready, before, keys, len(slots), first),
        out_shape=jax.ShapeDtypeStruct((sz.local_rows, sz.width), F32),
        in_specs=[SMEM] + [ANY] * (1 + len(keys) + len(slots)) + ([] if first else [VMEM]),
        out_specs=VMEM,
        scratch_shapes=job_scratch(sz),
        input_output_aliases={} if first else {len(args) - 1: 0},
        compiler_params=SMALL,
    )(*args)


def far_block(sz, row):
    far = jnp.where(row < sz.rows // 2, sz.rows - 1, 0)
    return far * sz.per_row + sz.per_row - 1


def inner_kernel(sz, pat, green, slot, factor, out, g_buf, sem):
    row, col = lax.axis_index("row"), lax.axis_index("col")
    a = far_block(sz, row)

    @pl.when(a // sz.half == col)
    def _():
        at = pl.multiple_of(lax.rem(a, sz.half) * sz.block, sz.block)
        pltpu.make_async_copy(green.at[0, :, pl.ds(at, sz.block)], g_buf, sem).start()

    @pl.when(a // sz.half != col)
    def _():
        pltpu.make_async_copy(slot, g_buf, sem).start()

    pltpu.make_async_copy(g_buf, g_buf, sem).wait()
    total = jnp.zeros((sz.width, sz.block), F32)
    for e in range(sz.per_row):
        at = pl.ds(e * sz.block, sz.block)
        kept = pat[col, row * sz.per_row + e] > 0
        part = lax.dot_general(factor[0, at, :], g_buf[at, :], (((0,), (0,)), ((), ())), preferred_element_type=F32)
        total = total + jnp.where(kept, part, 0.0)
    out[...] = total.astype(BF16)


def inner(sz, pattern, green, slot, factor):
    return pl.pallas_call(
        functools.partial(inner_kernel, sz),
        out_shape=jax.ShapeDtypeStruct((sz.width, sz.block), BF16),
        in_specs=[SMEM, ANY, ANY, VMEM],
        out_specs=VMEM,
        scratch_shapes=[pltpu.VMEM((sz.local_rows, sz.block), BF16), pltpu.SemaphoreType.DMA],
        compiler_params=SMALL,
        name="inner",
    )(pattern, *in_hbm([green, slot]), factor)


def late_diag_kernel(sz, ready, before, keys, n_slots, pat, weight, g_local, *refs):
    refs = list(refs)
    m_refs = {k: refs.pop(0) for k in keys}
    g_slots = [refs.pop(0) for _ in range(n_slots)]
    total_in, factor, dinv, far_term = (refs.pop(0) for _ in range(4))
    outs = [refs.pop(0) for _ in range(sz.cores)]
    total, diag = refs.pop(0), refs.pop(0)
    job, m_buf, g_buf, m_sem, g_sem = refs
    row, col = lax.axis_index("row"), lax.axis_index("col")
    core = lax.rem(lax.axis_index("pole"), sz.cores)

    away = sz.rows - 2
    for at_row, sign in ((1, 1), (sz.rows - 2, -1)):
        key = sign * away * sz.per_row + sz.per_row - 1

        @pl.when(row == at_row)
        def _(key=key):
            copy = pltpu.make_async_copy(m_refs[key], m_buf.at[0], m_sem.at[0])
            copy.start()
            copy.wait()

    inward = jnp.logical_or(row == 1, row == sz.rows - 2)
    a = far_block(sz, row)
    w = weight[0]
    diag[...] = jnp.zeros_like(diag)

    @pl.when(jnp.logical_and(inward, pat[col, a] > 0))
    def _():
        diag[...] -= w * jnp.dot(far_term[...], m_buf[0], preferred_element_type=F32)

    total[...] = total_in[...]
    product_jobs(sz, pat, ready, before, m_refs, g_local, g_slots, job, (m_buf, g_buf, m_sem, g_sem), total)
    for e in range(sz.per_row):
        at = pl.ds(e * sz.block, sz.block)

        @pl.when(pat[col, row * sz.per_row + e] > 0)
        def _(at=at):
            diag[...] -= w * lax.dot_general(
                factor[0, at, :], total[at, :].astype(BF16), (((0,), (0,)), ((), ())), preferred_element_type=F32)

    mine = pl.ds(pl.multiple_of(row * sz.count, sz.count), sz.count)
    diag[mine, :] += w * dinv[0].astype(F32)
    n = diag.shape[0] // sz.poles
    for dc, out in enumerate(outs):
        for x in range(sz.outer):
            q = x * sz.cores + lax.rem(core + dc, sz.cores)
            out[x * n:(x + 1) * n, :] = diag[pl.ds(pl.multiple_of(q * n, n), n), :].astype(out.dtype)


def late_diag(sz, ready, before, pattern, weight, green, m, slots, landed, total, factor, dinv, far_term):
    keys = list(m)
    args = [pattern, weight] + in_hbm([green] + [m[k] for k in keys])
    args += [v if s == landed else in_hbm([v])[0] for s, v in enumerate(slots)] + [total, factor, dinv, far_term]
    shapes = [jax.ShapeDtypeStruct((sz.block // sz.cores, sz.width), BF16 if i else F32) for i in range(sz.cores)]
    shapes.append(jax.ShapeDtypeStruct((sz.local_rows, sz.width), F32))
    return pl.pallas_call(
        functools.partial(late_diag_kernel, sz, ready, before, keys, len(slots)),
        out_shape=shapes,
        in_specs=[SMEM] * 2 + [ANY] * (1 + len(keys))
        + [VMEM if s == landed else ANY for s in range(len(slots))] + [VMEM] * 4,
        out_specs=[VMEM] * (sz.cores + 1),
        scratch_shapes=[pltpu.VMEM((sz.block, sz.width), F32)] + job_scratch(sz),
        compiler_params=SMALL,
        name="late_diag",
    )(*args)


def late_off_kernel(sz, ready, before, keys, n_slots, pat, weight, g_local, *refs):
    refs = list(refs)
    m_refs = {k: refs.pop(0) for k in keys}
    g_slots = [refs.pop(0) for _ in range(n_slots)]
    total_in = refs.pop(0)
    outs = [refs.pop(0) for _ in range(sz.cores)]
    total = refs.pop(0)
    job, m_buf, g_buf, m_sem, g_sem = refs
    row, col = lax.axis_index("row"), lax.axis_index("col")
    core = lax.rem(lax.axis_index("pole"), sz.cores)
    total[...] = total_in[...]
    product_jobs(sz, pat, ready, before, m_refs, g_local, g_slots, job, (m_buf, g_buf, m_sem, g_sem), total)
    w = weight[0]
    n = total.shape[0] // sz.poles
    for dc, out in enumerate(outs):
        for x in range(sz.outer):
            q = x * sz.cores + lax.rem(core + dc, sz.cores)
            kept = pat[col, row * sz.per_row + (q * n) // sz.block] > 0
            v = total[pl.ds(pl.multiple_of(q * n, n), n), :]
            out[x * n:(x + 1) * n, :] = jnp.where(kept, -w * v, 0.0).astype(out.dtype)


def late_off(sz, ready, before, pattern, weight, green, m, slots, total):
    keys = list(m)
    args = [pattern, weight] + in_hbm([green] + [m[k] for k in keys] + list(slots)) + [total]
    shapes = [jax.ShapeDtypeStruct((sz.local_rows // sz.cores, sz.width), BF16 if i else F32) for i in range(sz.cores)]
    return pl.pallas_call(
        functools.partial(late_off_kernel, sz, ready, before, keys, len(slots)),
        out_shape=shapes,
        in_specs=[SMEM] * 2 + [ANY] * (1 + len(keys) + len(slots)) + [VMEM],
        out_specs=[VMEM] * sz.cores,
        scratch_shapes=[pltpu.VMEM((sz.local_rows, sz.width), F32)] + job_scratch(sz),
        compiler_params=SMALL,
        name="late_off",
    )(*args)


def fold_kernel(group, n_in, axis, stride, keep, *refs):
    ins, outs = refs[:n_in], refs[n_in:]
    own, sends = outs[0], outs[1:]
    n = own.shape[0]
    me = lax.rem(lax.axis_index(axis) // stride, group)

    def part(d):
        at = pl.ds(pl.multiple_of(d * n, n), n)
        v = keep[at, :]
        for r in ins:
            v = v + r[at, :].astype(F32)
        return v

    for s, send in enumerate(sends):
        to = me ^ (s + 1) if group & (group - 1) == 0 else lax.rem(me + s + 1, group)
        send[...] = part(to).astype(BF16)
    own[...] = part(me)


def fold(group, axis, stride, keep, ins):
    n, width = keep.shape[0] // group, keep.shape[1]
    shapes = [jax.ShapeDtypeStruct((n, width), F32)] + [jax.ShapeDtypeStruct((n, width), BF16)] * (group - 1)
    return pl.pallas_call(
        functools.partial(fold_kernel, group, len(ins), axis, stride),
        out_shape=shapes,
        in_specs=[VMEM] * (1 + len(ins)),
        out_specs=[VMEM] * group,
        compiler_params=SMALL,
    )(keep, *ins)


def shifts(size, group, stride):
    perms = []
    for step in range(1, group):
        perm = []
        for i in range(size):
            d = (i // stride) % group
            to = d ^ step if group & (group - 1) == 0 else (d + step) % group
            perm.append((i, i + (to - d) * stride))
        perms.append(perm)
    return perms


def blocked(sz, green, factor, diag_inverse, pole_weight, pattern):
    block, per_row = sz.block, sz.per_row
    pattern = pattern.T
    fac = [factor[0, e * block:(e + 1) * block] for e in range(per_row)]
    swap = [(0, 1), (1, 0)]

    fixed = max(sz.half - 1, 1)
    slots = []
    for s in range(fixed):
        sent = pick(sz, s, pattern, green)
        slots.append(lax.ppermute(sent, "col", swap))

    m = {e: fac[e] for e in range(per_row)}
    for e in range(per_row):
        a = b = fac[e]
        for step in range(1, sz.rows):
            m[-step * per_row + e] = a = lax.ppermute(a, "row", [(i, i + 1) for i in range(step - 1, sz.rows - 1)])
            m[step * per_row + e] = b = lax.ppermute(b, "row", [(i + 1, i) for i in range(sz.rows - step)])

    def upto(dist, last_e):
        return {k: v for k, v in m.items() if abs(k // per_row) < dist or (abs(k // per_row) == dist and k % per_row <= last_e)}

    far = sz.rows - 1
    bounds = [(far - 2, per_row - 1, 0), (far - 1, per_row - 1, fixed - 2), (far, per_row - 2, fixed - 2)]
    far_term = inner(sz, pattern, green, slots[0], factor)
    far_term = lax.ppermute(far_term, "row", [(0, 1), (far, far - 1)])

    def part(i, total):
        dist, last_e, s = bounds[i]
        return early(sz, bounds[i], bounds[i - 1] if i else None, pattern, green,
                     upto(dist, last_e), slots[:s + 1], total)

    total = part(1, part(0, None))
    extra = []
    if sz.half > fixed:
        full = jnp.bool_(False)
        for c in range(sz.cols):
            other = (1 - c) * sz.half
            full = jnp.logical_or(full, jnp.all(pattern[c, other:other + sz.half] > 0))

        def more(g):
            return lax.ppermute(pick(sz, fixed, pattern, g), "col", swap)

        full, total = lax.optimization_barrier((full, total))
        got = lax.cond(full, more, lambda g: jnp.zeros((sz.local_rows, block), BF16), green)
        got, total = lax.optimization_barrier((got, total))
        extra.append(got)
    total = part(2, total)
    near = (far, per_row - 2, sz.half)
    *out, total = late_diag(sz, near, bounds[2], pattern, pole_weight, green, upto(far, per_row - 2),
                            slots + extra, fixed - 1, total, factor, diag_inverse, far_term)
    last = (far, per_row - 1, sz.half)
    only = {k: v for k, v in m.items() if abs(k // per_row) == far and k % per_row == per_row - 1}
    off_out = late_off(sz, last, near, pattern, pole_weight, green, only, slots + extra, total)

    def swapped(axis, sends, perms):
        ins = []
        for v, perm in zip(sends, perms):
            ins.append(lax.ppermute(v, axis, perm))
        return ins

    diag, *sends = out
    diag_in = swapped("pole", sends, shifts(sz.poles, sz.cores, 1))
    diag, *sends = fold(sz.outer, "pole", sz.cores, diag, diag_in)
    diag_in = swapped("pole", sends, shifts(sz.poles, sz.outer, sz.cores))
    off, *sends = off_out
    off_in = swapped("pole", sends, shifts(sz.poles, sz.cores, 1))
    off, *sends = fold(sz.outer, "pole", sz.cores, off, off_in)
    off_in = swapped("pole", sends, shifts(sz.poles, sz.outer, sz.cores))
    diag, *sends = fold(sz.rows, "row", 1, diag, diag_in)
    diag_in = swapped("row", sends, shifts(sz.rows, sz.rows, 1))
    for v in off_in:
        off = off + v.astype(F32)
    for v in diag_in:
        diag = diag + v.astype(F32)
    return off, diag


def make_body(mesh):
    def body(green, factor, diag_inverse, pole_weight, pattern):
        sz = Sizes(mesh, green, factor, diag_inverse, pattern)
        fits = sz.cols == 2 and sz.level == 1 and sz.cores == 2 and sz.rows >= 4 and sz.block % (sz.local_rows // sz.poles) == 0 and sz.per_row >= 2 and sz.half >= 3
        if not fits:
            return generic(sz, green, factor, diag_inverse, pole_weight, pattern)
        return blocked(sz, green, factor, diag_inverse, pole_weight, pattern)

    return body


def solution(mesh):
    in_specs = (
        P("pole", "row", "col"),
        P("pole", "row", "col"),
        P("pole", "row", "col"),
        P("pole"),
        P(),
    )
    out_specs = (P(("row", "pole"), "col"), P(("pole", "row"), "col"))
    return jax.shard_map(make_body(mesh), mesh=mesh, in_specs=in_specs, out_specs=out_specs, check_vma=False)
```

```python
import functools

import jax
import jax.numpy as jnp
from jax import lax
from jax.experimental import pallas as pl
from jax.experimental.pallas import tpu as pltpu
from jax.sharding import PartitionSpec as P


VMEM = pl.BlockSpec(memory_space=pltpu.VMEM)
SMEM = pl.BlockSpec(memory_space=pltpu.SMEM)
ANY = pl.BlockSpec(memory_space=pltpu.HBM)
SMALL = pltpu.CompilerParams(vmem_limit_bytes=12 * 2**20)
F32 = jnp.float32
BF16 = jnp.bfloat16


class Sizes:
    def __init__(self, mesh, green, factor, diag_inverse, pattern):
        self.poles, self.rows, self.cols = (mesh.shape[a] for a in ("pole", "row", "col"))
        self.local_rows, self.k_local = green.shape[1], green.shape[2]
        self.width = factor.shape[2]
        self.anc, supers = pattern.shape
        self.block = self.local_rows * self.rows // self.anc
        self.per_row = self.local_rows // self.block
        self.half = self.k_local // self.block
        self.level = supers // self.cols
        self.count = diag_inverse.shape[1]
        self.cores = 2 if self.poles % 2 == 0 else 1
        self.outer = self.poles // self.cores


def swap_sum(part, axis, size, group, stride, held_as):
    at = lax.axis_index(axis)
    digit = (at // stride) % group
    total = lax.dynamic_index_in_dim(part, digit, 0, keepdims=False)
    for step in range(1, group):
        perm = []
        for i in range(size):
            d = (i // stride) % group
            perm.append((i, i + ((d + step) % group - d) * stride))
        to = (digit + step) % group
        send = lax.dynamic_index_in_dim(part, to, 0, keepdims=False).astype(held_as)
        total = total + lax.ppermute(send, axis, perm).astype(F32)
    return total


def generic(sz, green, factor, diag_inverse, pole_weight, pattern):
    block, per_row, cols = sz.block, sz.per_row, sz.width
    row_at = lax.axis_index("row")
    col_at = lax.axis_index("col")
    pattern_f = pattern.astype(F32)
    here = lax.dynamic_slice(pattern_f, (0, col_at * sz.level), (sz.anc, sz.level))
    keep = jnp.repeat(here, block, axis=1)
    own_keep = lax.dynamic_slice_in_dim(keep, row_at * per_row, per_row, 0)
    weight = pole_weight[0]
    gl = green[0]
    fac = factor[0].reshape(per_row, block, cols)
    got = {}
    for shift in range(1, sz.cols):
        perm = [(i, (i + shift) % sz.cols) for i in range(sz.cols)]
        for j in range(sz.half):
            got[shift, j] = lax.ppermute(gl[:, j * block:(j + 1) * block], "col", perm)
    right = [(i, i + 1) for i in range(sz.rows - 1)]
    left = [(i + 1, i) for i in range(sz.rows - 1)]
    blocks = {(0, e): fac[e] for e in range(per_row)}
    from_left, from_right = {}, {}
    for e in range(per_row):
        a = b = fac[e]
        for step in range(1, sz.rows):
            from_left[step, e] = a = lax.ppermute(a, "row", right)
            from_right[step, e] = b = lax.ppermute(b, "row", left)
    for step in range(1, sz.rows):
        for e in range(per_row):
            blocks[step, e] = jnp.where(row_at >= step, from_left[step, e], from_right[sz.rows - step, e])
    stacked = jnp.stack([blocks[s, e] for s in range(sz.rows) for e in range(per_row)])

    def factor_of(a):
        at = ((row_at - a // per_row) % sz.rows) * per_row + a % per_row
        kept = lax.dynamic_index_in_dim(keep, a, 0).astype(BF16)
        return lax.dynamic_index_in_dim(stacked, at, 0, keepdims=False) * kept

    product = jnp.zeros((sz.local_rows, cols), F32)
    for shift in range(sz.cols):
        for j in range(sz.half):
            src = (col_at - shift) % sz.cols
            g = gl[:, j * block:(j + 1) * block] if shift == 0 else got[shift, j]
            product += jnp.dot(g, factor_of(src * sz.half + j), preferred_element_type=F32)
    product = product.reshape(per_row, block, cols) * own_keep[:, None, :]
    update = product.astype(BF16).reshape(sz.local_rows, sz.level, block)
    masked = (fac * own_keep.astype(BF16)[:, None, :]).reshape(sz.local_rows, sz.level, block)
    cross = jnp.einsum("rka,rkb->akb", masked, update, preferred_element_type=F32).reshape(block, cols)
    diag = -weight * cross
    mine = lax.dynamic_slice_in_dim(diag, row_at * sz.count, sz.count, 0)
    mine = mine + weight * diag_inverse[0].astype(F32)
    diag = lax.dynamic_update_slice_in_dim(diag, mine, row_at * sz.count, 0)
    off = -weight * product.reshape(sz.local_rows, cols)
    res = []
    for x in (diag, off):
        r = x.shape[0] // sz.poles
        x = x.reshape(sz.outer, sz.cores, r, cols).transpose(1, 0, 2, 3)
        x = swap_sum(x, "pole", sz.poles, sz.cores, 1, BF16)
        res.append(swap_sum(x, "pole", sz.poles, sz.outer, sz.cores, BF16))
    diag, off = res
    return off, swap_sum(diag.reshape(sz.rows, -1, cols), "row", sz.rows, sz.rows, 1, BF16)


def swap_ranks(sz, pat, row, to):
    base = (1 - to) * sz.half
    need, dist = [], []
    for j in range(sz.half):
        need.append(pat[to, base + j])
        dist.append(jnp.abs((base + j) // sz.per_row - row))
    rank = []
    for j in range(sz.half):
        n = jnp.int32(0)
        for i in range(sz.half):
            if i != j:
                before = dist[i] > dist[j] if i < j else dist[i] >= dist[j]
                n = n + jnp.where(before, need[i], 0)
        rank.append(n)
    return need, rank


def pick_kernel(sz, slot, parts, pat, green, out, buf, in_sem, out_sem):
    need, rank = swap_ranks(sz, pat, lax.axis_index("row"), 1 - lax.axis_index("col"))
    at = jnp.int32(0)
    for j in range(sz.half):
        at = jnp.where(jnp.logical_and(need[j] > 0, rank[j] == slot), j, at)
    at = pl.multiple_of(at * sz.block, sz.block)
    n = sz.local_rows // parts
    ins, outs = [], []
    for i in range(parts):
        ins.append(pltpu.make_async_copy(green.at[0, pl.ds(i * n, n), pl.ds(at, sz.block)], buf.at[i], in_sem.at[i]))
        outs.append(pltpu.make_async_copy(buf.at[i], out.at[pl.ds(i * n, n)], out_sem.at[i]))
        ins[i].start()
    for i in range(parts):
        ins[i].wait()
        outs[i].start()
    for i in range(parts):
        outs[i].wait()


def pick(sz, slot, pattern, green):
    parts = 4
    return pl.pallas_call(
        functools.partial(pick_kernel, sz, slot, parts),
        out_shape=jax.ShapeDtypeStruct((sz.local_rows, sz.block), BF16),
        in_specs=[SMEM, ANY],
        out_specs=ANY,
        scratch_shapes=[
            pltpu.VMEM((parts, sz.local_rows // parts, sz.block), BF16),
            pltpu.SemaphoreType.DMA((parts,)),
            pltpu.SemaphoreType.DMA((parts,)),
        ],
        compiler_params=SMALL,
    )(pattern, *in_hbm([green]))


def product_jobs(sz, pat, ready, before, m_refs, g_local, g_slots, job, bufs, total):
    m_buf, g_buf, m_sem, g_sem = bufs
    row, col = lax.axis_index("row"), lax.axis_index("col")
    _, rank = swap_ranks(sz, pat, row, col)

    def inside(bound, dist, e, slot):
        if bound is None:
            return jnp.bool_(False)
        d, last_e, s = bound
        near = jnp.logical_or(dist < d, jnp.logical_and(dist == d, e <= last_e))
        return jnp.logical_and(near, slot <= s)

    count = jnp.int32(0)
    for a in range(sz.anc):
        away = a // sz.per_row - row
        dist, e = jnp.abs(away), a % sz.per_row
        local = (a // sz.half) == col
        slot = jnp.where(local, -1, rank[a % sz.half])
        todo = jnp.logical_and(inside(ready, dist, e, slot), jnp.logical_not(inside(before, dist, e, slot)))
        todo = jnp.logical_and(todo, pat[col, a] > 0)

        @pl.when(todo)
        def _(a=a, count=count, slot=slot, away=away):
            job[0, count] = away * sz.per_row + a % sz.per_row
            job[1, count] = slot
            job[2, count] = a % sz.half

        count = count + jnp.where(todo, 1, 0)

    def fetch(n, into):
        for key, ref in m_refs.items():
            @pl.when(job[0, n] == key)
            def _(ref=ref):
                pltpu.make_async_copy(ref, m_buf.at[into], m_sem.at[into]).start()

        @pl.when(job[1, n] < 0)
        def _():
            at = pl.multiple_of(job[2, n] * sz.block, sz.block)
            pltpu.make_async_copy(g_local.at[0, :, pl.ds(at, sz.block)], g_buf.at[into], g_sem.at[into]).start()

        for s, ref in enumerate(g_slots):
            @pl.when(job[1, n] == s)
            def _(ref=ref):
                pltpu.make_async_copy(ref, g_buf.at[into], g_sem.at[into]).start()

    @pl.when(count > 0)
    def _():
        fetch(0, 0)

    def step(n, carry):
        now = lax.rem(n, 2)

        @pl.when(n + 1 < count)
        def _():
            fetch(n + 1, 1 - now)

        pltpu.make_async_copy(m_buf.at[now], m_buf.at[now], m_sem.at[now]).wait()
        pltpu.make_async_copy(g_buf.at[now], g_buf.at[now], g_sem.at[now]).wait()
        total[...] += jnp.dot(g_buf[now], m_buf[now], preferred_element_type=F32)
        return carry

    lax.fori_loop(0, count, step, 0)


def in_hbm(arrays):
    return [pltpu.with_memory_space_constraint(a, pltpu.HBM) for a in arrays]


def job_scratch(sz):
    return [
        pltpu.SMEM((3, sz.anc), jnp.int32),
        pltpu.VMEM((2, sz.block, sz.width), BF16),
        pltpu.VMEM((2, sz.local_rows, sz.block), BF16),
        pltpu.SemaphoreType.DMA((2,)),
        pltpu.SemaphoreType.DMA((2,)),
    ]


def early_kernel(sz, ready, before, keys, n_slots, first, pat, g_local, *refs):
    refs = list(refs)
    m_refs = {k: refs.pop(0) for k in keys}
    g_slots = [refs.pop(0) for _ in range(n_slots)]
    total_in = None if first else refs.pop(0)
    out = refs.pop(0)
    job, m_buf, g_buf, m_sem, g_sem = refs
    if first:
        out[...] = jnp.zeros_like(out)
    else:
        out[...] = total_in[...]
    product_jobs(sz, pat, ready, before, m_refs, g_local, g_slots, job, (m_buf, g_buf, m_sem, g_sem), out)


def early(sz, ready, before, pattern, green, m, slots, total):
    keys = list(m)
    first = total is None
    args = [pattern] + in_hbm([green] + [m[k] for k in keys] + list(slots)) + ([] if first else [total])
    return early_call(sz, ready, before, keys, slots, first, args)


def early_call(sz, ready, before, keys, slots, first, args):
    return pl.pallas_call(
        functools.partial(early_kernel, sz, ready, before, keys, len(slots), first),
        out_shape=jax.ShapeDtypeStruct((sz.local_rows, sz.width), F32),
        in_specs=[SMEM] + [ANY] * (1 + len(keys) + len(slots)) + ([] if first else [VMEM]),
        out_specs=VMEM,
        scratch_shapes=job_scratch(sz),
        input_output_aliases={} if first else {len(args) - 1: 0},
        compiler_params=SMALL,
    )(*args)


def far_block(sz, row):
    far = jnp.where(row < sz.rows // 2, sz.rows - 1, 0)
    return far * sz.per_row + sz.per_row - 1


def inner_kernel(sz, pat, green, slot, factor, out, g_buf, sem):
    row, col = lax.axis_index("row"), lax.axis_index("col")
    a = far_block(sz, row)

    @pl.when(a // sz.half == col)
    def _():
        at = pl.multiple_of(lax.rem(a, sz.half) * sz.block, sz.block)
        pltpu.make_async_copy(green.at[0, :, pl.ds(at, sz.block)], g_buf, sem).start()

    @pl.when(a // sz.half != col)
    def _():
        pltpu.make_async_copy(slot, g_buf, sem).start()

    pltpu.make_async_copy(g_buf, g_buf, sem).wait()
    total = jnp.zeros((sz.width, sz.block), F32)
    for e in range(sz.per_row):
        at = pl.ds(e * sz.block, sz.block)
        kept = pat[col, row * sz.per_row + e] > 0
        part = lax.dot_general(factor[0, at, :], g_buf[at, :], (((0,), (0,)), ((), ())), preferred_element_type=F32)
        total = total + jnp.where(kept, part, 0.0)
    out[...] = total.astype(BF16)


def inner(sz, pattern, green, slot, factor):
    return pl.pallas_call(
        functools.partial(inner_kernel, sz),
        out_shape=jax.ShapeDtypeStruct((sz.width, sz.block), BF16),
        in_specs=[SMEM, ANY, ANY, VMEM],
        out_specs=VMEM,
        scratch_shapes=[pltpu.VMEM((sz.local_rows, sz.block), BF16), pltpu.SemaphoreType.DMA],
        compiler_params=SMALL,
        name="inner",
    )(pattern, *in_hbm([green, slot]), factor)


def late_diag_kernel(sz, ready, before, keys, n_slots, pat, weight, g_local, *refs):
    refs = list(refs)
    m_refs = {k: refs.pop(0) for k in keys}
    g_slots = [refs.pop(0) for _ in range(n_slots)]
    total_in, factor, dinv, far_term = (refs.pop(0) for _ in range(4))
    outs = [refs.pop(0) for _ in range(sz.cores)]
    total, diag = refs.pop(0), refs.pop(0)
    job, m_buf, g_buf, m_sem, g_sem = refs
    row, col = lax.axis_index("row"), lax.axis_index("col")
    core = lax.rem(lax.axis_index("pole"), sz.cores)

    away = sz.rows - 2
    for at_row, sign in ((1, 1), (sz.rows - 2, -1)):
        key = sign * away * sz.per_row + sz.per_row - 1

        @pl.when(row == at_row)
        def _(key=key):
            copy = pltpu.make_async_copy(m_refs[key], m_buf.at[0], m_sem.at[0])
            copy.start()
            copy.wait()

    inward = jnp.logical_or(row == 1, row == sz.rows - 2)
    a = far_block(sz, row)
    w = weight[0]
    diag[...] = jnp.zeros_like(diag)

    @pl.when(jnp.logical_and(inward, pat[col, a] > 0))
    def _():
        diag[...] -= w * jnp.dot(far_term[...], m_buf[0], preferred_element_type=F32)

    total[...] = total_in[...]
    product_jobs(sz, pat, ready, before, m_refs, g_local, g_slots, job, (m_buf, g_buf, m_sem, g_sem), total)
    for e in range(sz.per_row):
        at = pl.ds(e * sz.block, sz.block)

        @pl.when(pat[col, row * sz.per_row + e] > 0)
        def _(at=at):
            diag[...] -= w * lax.dot_general(
                factor[0, at, :], total[at, :].astype(BF16), (((0,), (0,)), ((), ())), preferred_element_type=F32)

    mine = pl.ds(pl.multiple_of(row * sz.count, sz.count), sz.count)
    diag[mine, :] += w * dinv[0].astype(F32)
    n = diag.shape[0] // sz.poles
    for dc, out in enumerate(outs):
        for x in range(sz.outer):
            q = x * sz.cores + lax.rem(core + dc, sz.cores)
            out[x * n:(x + 1) * n, :] = diag[pl.ds(pl.multiple_of(q * n, n), n), :].astype(out.dtype)


def late_diag(sz, ready, before, pattern, weight, green, m, slots, landed, total, factor, dinv, far_term):
    keys = list(m)
    args = [pattern, weight] + in_hbm([green] + [m[k] for k in keys])
    args += [v if s == landed else in_hbm([v])[0] for s, v in enumerate(slots)] + [total, factor, dinv, far_term]
    shapes = [jax.ShapeDtypeStruct((sz.block // sz.cores, sz.width), BF16 if i else F32) for i in range(sz.cores)]
    shapes.append(jax.ShapeDtypeStruct((sz.local_rows, sz.width), F32))
    return pl.pallas_call(
        functools.partial(late_diag_kernel, sz, ready, before, keys, len(slots)),
        out_shape=shapes,
        in_specs=[SMEM] * 2 + [ANY] * (1 + len(keys))
        + [VMEM if s == landed else ANY for s in range(len(slots))] + [VMEM] * 4,
        out_specs=[VMEM] * (sz.cores + 1),
        scratch_shapes=[pltpu.VMEM((sz.block, sz.width), F32)] + job_scratch(sz),
        compiler_params=SMALL,
        name="late_diag",
    )(*args)


def late_off_kernel(sz, ready, before, keys, n_slots, pat, weight, g_local, *refs):
    refs = list(refs)
    m_refs = {k: refs.pop(0) for k in keys}
    g_slots = [refs.pop(0) for _ in range(n_slots)]
    total_in = refs.pop(0)
    outs = [refs.pop(0) for _ in range(sz.cores)]
    total = refs.pop(0)
    job, m_buf, g_buf, m_sem, g_sem = refs
    row, col = lax.axis_index("row"), lax.axis_index("col")
    core = lax.rem(lax.axis_index("pole"), sz.cores)
    total[...] = total_in[...]
    product_jobs(sz, pat, ready, before, m_refs, g_local, g_slots, job, (m_buf, g_buf, m_sem, g_sem), total)
    w = weight[0]
    n = total.shape[0] // sz.poles
    for dc, out in enumerate(outs):
        for x in range(sz.outer):
            q = x * sz.cores + lax.rem(core + dc, sz.cores)
            kept = pat[col, row * sz.per_row + (q * n) // sz.block] > 0
            v = total[pl.ds(pl.multiple_of(q * n, n), n), :]
            out[x * n:(x + 1) * n, :] = jnp.where(kept, -w * v, 0.0).astype(out.dtype)


def late_off(sz, ready, before, pattern, weight, green, m, slots, total):
    keys = list(m)
    args = [pattern, weight] + in_hbm([green] + [m[k] for k in keys] + list(slots)) + [total]
    shapes = [jax.ShapeDtypeStruct((sz.local_rows // sz.cores, sz.width), BF16 if i else F32) for i in range(sz.cores)]
    return pl.pallas_call(
        functools.partial(late_off_kernel, sz, ready, before, keys, len(slots)),
        out_shape=shapes,
        in_specs=[SMEM] * 2 + [ANY] * (1 + len(keys) + len(slots)) + [VMEM],
        out_specs=[VMEM] * sz.cores,
        scratch_shapes=[pltpu.VMEM((sz.local_rows, sz.width), F32)] + job_scratch(sz),
        compiler_params=SMALL,
        name="late_off",
    )(*args)


def fold_kernel(group, n_in, axis, stride, keep, *refs):
    ins, outs = refs[:n_in], refs[n_in:]
    own, sends = outs[0], outs[1:]
    n = own.shape[0]
    me = lax.rem(lax.axis_index(axis) // stride, group)

    def part(d):
        at = pl.ds(pl.multiple_of(d * n, n), n)
        v = keep[at, :]
        for r in ins:
            v = v + r[at, :].astype(F32)
        return v

    for s, send in enumerate(sends):
        to = me ^ (s + 1) if group & (group - 1) == 0 else lax.rem(me + s + 1, group)
        send[...] = part(to).astype(BF16)
    own[...] = part(me)


def fold(group, axis, stride, keep, ins):
    n, width = keep.shape[0] // group, keep.shape[1]
    shapes = [jax.ShapeDtypeStruct((n, width), F32)] + [jax.ShapeDtypeStruct((n, width), BF16)] * (group - 1)
    return pl.pallas_call(
        functools.partial(fold_kernel, group, len(ins), axis, stride),
        out_shape=shapes,
        in_specs=[VMEM] * (1 + len(ins)),
        out_specs=[VMEM] * group,
        compiler_params=SMALL,
    )(keep, *ins)


def shifts(size, group, stride):
    perms = []
    for step in range(1, group):
        perm = []
        for i in range(size):
            d = (i // stride) % group
            to = d ^ step if group & (group - 1) == 0 else (d + step) % group
            perm.append((i, i + (to - d) * stride))
        perms.append(perm)
    return perms


def blocked(sz, green, factor, diag_inverse, pole_weight, pattern):
    block, per_row = sz.block, sz.per_row
    pattern = pattern.T
    fac = [factor[0, e * block:(e + 1) * block] for e in range(per_row)]
    swap = [(0, 1), (1, 0)]

    fixed = max(sz.half - 1, 1)
    slots = []
    for s in range(fixed):
        sent = pick(sz, s, pattern, green)
        slots.append(lax.ppermute(sent, "col", swap))

    m = {e: fac[e] for e in range(per_row)}
    for e in range(per_row):
        a = b = fac[e]
        for step in range(1, sz.rows):
            m[-step * per_row + e] = a = lax.ppermute(a, "row", [(i, i + 1) for i in range(step - 1, sz.rows - 1)])
            m[step * per_row + e] = b = lax.ppermute(b, "row", [(i + 1, i) for i in range(sz.rows - step)])

    def upto(dist, last_e):
        return {k: v for k, v in m.items() if abs(k // per_row) < dist or (abs(k // per_row) == dist and k % per_row <= last_e)}

    far = sz.rows - 1
    bounds = [(far - 2, per_row - 1, 0), (far - 1, per_row - 1, fixed - 2), (far, per_row - 2, fixed - 2)]
    far_term = inner(sz, pattern, green, slots[0], factor)
    far_term = lax.ppermute(far_term, "row", [(0, 1), (far, far - 1)])

    def part(i, total):
        dist, last_e, s = bounds[i]
        return early(sz, bounds[i], bounds[i - 1] if i else None, pattern, green,
                     upto(dist, last_e), slots[:s + 1], total)

    total = part(1, part(0, None))
    extra = []
    if sz.half > fixed:
        full = jnp.bool_(False)
        for c in range(sz.cols):
            other = (1 - c) * sz.half
            full = jnp.logical_or(full, jnp.all(pattern[c, other:other + sz.half] > 0))

        def more(g):
            return lax.ppermute(pick(sz, fixed, pattern, g), "col", swap)

        full, total = lax.optimization_barrier((full, total))
        got = lax.cond(full, more, lambda g: jnp.zeros((sz.local_rows, block), BF16), green)
        got, total = lax.optimization_barrier((got, total))
        extra.append(got)
    total = part(2, total)
    near = (far, per_row - 2, sz.half)
    *out, total = late_diag(sz, near, bounds[2], pattern, pole_weight, green, upto(far, per_row - 2),
                            slots + extra, fixed - 1, total, factor, diag_inverse, far_term)
    last = (far, per_row - 1, sz.half)
    only = {k: v for k, v in m.items() if abs(k // per_row) == far and k % per_row == per_row - 1}
    off_out = late_off(sz, last, near, pattern, pole_weight, green, only, slots + extra, total)

    def swapped(axis, sends, perms):
        ins = []
        for v, perm in zip(sends, perms):
            ins.append(lax.ppermute(v, axis, perm))
        return ins

    diag, *sends = out
    diag_in = swapped("pole", sends, shifts(sz.poles, sz.cores, 1))
    diag, *sends = fold(sz.outer, "pole", sz.cores, diag, diag_in)
    diag_in = swapped("pole", sends, shifts(sz.poles, sz.outer, sz.cores))
    off, *sends = off_out
    off_in = swapped("pole", sends, shifts(sz.poles, sz.cores, 1))
    off, *sends = fold(sz.outer, "pole", sz.cores, off, off_in)
    off_in = swapped("pole", sends, shifts(sz.poles, sz.outer, sz.cores))
    diag, *sends = fold(sz.rows, "row", 1, diag, diag_in)
    diag_in = swapped("row", sends, shifts(sz.rows, sz.rows, 1))
    return last_sums(off, off_in, diag, diag_in)


def last_kernel(n_off, n_diag, *refs):
    off, *off_in = refs[:n_off]
    diag, *diag_in = refs[n_off:n_off + n_diag]
    for own, ins, out in ((off, off_in, refs[-2]), (diag, diag_in, refs[-1])):
        v = own[...]
        for r in ins:
            v = v + r[...].astype(F32)
        out[...] = v


def last_sums(off, off_in, diag, diag_in):
    return pl.pallas_call(
        functools.partial(last_kernel, 1 + len(off_in), 1 + len(diag_in)),
        out_shape=[jax.ShapeDtypeStruct(v.shape, F32) for v in (off, diag)],
        in_specs=[VMEM] * (2 + len(off_in) + len(diag_in)),
        out_specs=[VMEM] * 2,
        compiler_params=SMALL,
        name="last_sums",
    )(off, *off_in, diag, *diag_in)


def make_body(mesh):
    def body(green, factor, diag_inverse, pole_weight, pattern):
        sz = Sizes(mesh, green, factor, diag_inverse, pattern)
        fits = sz.cols == 2 and sz.level == 1 and sz.cores == 2 and sz.rows >= 4 and sz.block % (sz.local_rows // sz.poles) == 0 and sz.per_row >= 2 and sz.half >= 3
        if not fits:
            return generic(sz, green, factor, diag_inverse, pole_weight, pattern)
        return blocked(sz, green, factor, diag_inverse, pole_weight, pattern)

    return body


def solution(mesh):
    in_specs = (
        P("pole", "row", "col"),
        P("pole", "row", "col"),
        P("pole", "row", "col"),
        P("pole"),
        P(),
    )
    out_specs = (P(("row", "pole"), "col"), P(("pole", "row"), "col"))
    return jax.shard_map(make_body(mesh), mesh=mesh, in_specs=in_specs, out_specs=out_specs, check_vma=False)
```
